32 devices in a mesh: rows: 4 (over z), cols: 8 (over y, x, core).
Axes of the slice: x: 2, y: 2, z: 4, core: 2. Of those that a mesh axis runs over, the one named last changes fastest.
Arguments:
- pivot_rhs: float32 [4, 4096, 1024], P(None, 'cols'), may hold values from -6 to 6
- bound_sol: bfloat16 [16384, 1024], P('rows'), may hold values from -6 to 6
- border_tiles: bfloat16 [16384, 4, 4096], P('rows', None, 'cols'), may hold values from -0.046875 to 0.046875
- lower_tiles: bfloat16 [6, 4096, 4096], P(None, 'rows', 'cols'), may hold values from -0.09375 to 0.09375
- inverse_diag: bfloat16 [4, 4096, 4096], P(None, 'cols', 'rows'), may hold values from -0.09375 to 0.09375
- owner_map: int32 [32, 512, 1], P(('rows', 'cols')), may hold values from 0 to 31; in each aligned block of 512 rows (0 to 511, 512 to 1023, ..., all dimensions but the last counted through in order) at most 32 rows name the same one
Outputs:
- child_rows: float32 [32768, 1024], P(('rows', 'cols'))
The draws below stay inside these ranges and needn't reach their ends.
Inputs may be any that keep to these rules, and one draw needn't show every extreme that they name: `owner_map`: among the rows of one device (one index of the first dimension), no owner is named more than 32 times, a bound that some block reaches; every owner is named somewhere.
All inputs are finite; a program needn't handle non-finite values.
Results may differ from the reference program's by a relative error of at most 0.008.
Values may be sent and summed in bfloat16 or wider, within the bound.
A program may use at most 128 MiB of HBM per device.

```python
import math
import jax
import jax.numpy as jnp
import numpy as np
from jax import lax

NB = 4
BS = 4096
BND = 16384
NRHS = 1024
NPAIR = 6
ROWS_DEV = 512
MOST = 32
DEVICES = 32


def block_scale(rng, dims, split, smallest, largest):
    gain = 1.0
    for position, parts in split:
        steps = jax.random.uniform(jax.random.fold_in(jax.random.fold_in(rng, 6), position), (parts,), jnp.float32, smallest / len(split), largest / len(split))
        gain = gain * jnp.repeat(jnp.exp(steps), dims[position] // parts).reshape((-1,) + (1,) * (len(dims) - 1 - position))
    return gain


def shared_out(key, own, number, rows, amount, top, bound, slope):
    sequence = jax.random.permutation(key, amount)
    packed, ordinary = shares(amount, rows * top, bound, slope, True), shares(amount, rows * top, bound, slope, False)
    places = jnp.arange(amount)

    def named(tallies, offset_by):
        used = int((tallies > 0).sum())
        fixed = max(1, used // 4)
        moved = fixed + (places - fixed + offset_by * (used - fixed)) % max(1, amount - fixed)
        return jnp.zeros((amount,), jnp.int32).at[sequence[jnp.where(places < fixed, places, moved)]].set(jnp.asarray(tallies, jnp.int32))

    tallies = jnp.where(number % 4 == 0, named(packed, number // 4), named(ordinary, number - number // 4 - 1))
    mixed = jax.random.permutation(jax.random.fold_in(own, 3), amount)
    donor, sink = mixed[0:amount // 2 * 2:2], mixed[1:amount // 2 * 2:2]
    room = jnp.minimum(tallies[donor] - 1, bound - tallies[sink]) // 2
    room = jnp.where((donor == sequence[0]) | (sink == sequence[0]) | (tallies[sink] == 0), 0, jnp.maximum(room, 0))
    moved = jax.random.randint(jax.random.fold_in(own, 4), (amount // 2,), 0, 1 << 20) % (room + 1)
    tallies = tallies.at[donor].add(-moved).at[sink].add(moved)
    labels = jnp.searchsorted(jnp.cumsum(tallies), jnp.arange(rows * top), side="right").astype(jnp.int32)
    listing = labels.reshape(top, rows).T
    listing = listing[jax.random.permutation(jax.random.fold_in(own, 1), rows)]
    offset_by = jax.random.randint(jax.random.fold_in(own, 2), (rows, 1), 0, top)
    return jnp.take_along_axis(listing, (jnp.arange(top)[None, :] + offset_by) % top, axis=1)


def shares(count, total, most, lean, full):
    portions = [(1 << 20) // math.isqrt(rank ** lean) + 1 for rank in range(1, count + 1)]
    largest = most if full else min(most, max(-(-total // count), total * portions[0] // sum(portions)))
    least = 1 if total - largest >= count - 1 else 0
    counts, rest = [largest] + [least] * (count - 1), total - largest - least * (count - 1)
    while rest > 0:
        candidates = [i for i in range(1, count) if counts[i] < largest] or [i for i in range(1, count) if counts[i] < most]
        mass, budget = sum([portions[i] for i in candidates]), rest
        for i in candidates:
            addition = min(most - counts[i], max(1, budget * portions[i] // mass), rest)
            counts[i] = counts[i] + addition
            rest = rest - addition
    return np.array(counts)


def bell_draw(rng, extent, spread, bound, split=(), held_as=jnp.bfloat16):
    entries = jax.random.normal(rng, extent, jnp.float32) * spread
    if len(split) > 0:
        entries = block_scale(rng, extent, split, -0.22, 0.18) * entries
    return jnp.clip(entries, min=-bound, max=bound).astype(held_as)


def setup_inputs(seed: int = 0) -> dict:
    seeds = jax.random.split(jax.random.key(seed), 7)
    pivot_rhs = bell_draw(seeds[0], (NB, BS, NRHS), 1.0, 6.0, ((1, 8),), jnp.float32)
    bound_sol = bell_draw(seeds[1], (BND, NRHS), 1.0, 6.0, ((0, 4),))
    border_tiles = bell_draw(seeds[2], (BND, NB, BS), BND ** -0.5, 0.046875, ((0, 4), (2, 8)))
    lower_tiles = bell_draw(seeds[3], (NPAIR, BS, BS), BS ** -0.5, 0.09375, ((1, 4), (2, 8)))
    inverse_diag = bell_draw(seeds[4], (NB, BS, BS), BS ** -0.5, 0.09375, ((1, 8), (2, 4)))
    owner_map_keys = jax.random.split(jax.random.fold_in(seeds[5], 1), DEVICES * ROWS_DEV // ROWS_DEV)
    owner_map_turns = jax.random.permutation(jax.random.fold_in(seeds[5], 3), DEVICES * ROWS_DEV // ROWS_DEV)
    owner_map = jax.vmap(lambda own, number: shared_out(jax.random.fold_in(seeds[5], 2), own, number, ROWS_DEV, DEVICES, 1, MOST, 2))(owner_map_keys, owner_map_turns).reshape((DEVICES, ROWS_DEV, 1))
    return {"pivot_rhs": pivot_rhs, "bound_sol": bound_sol, "border_tiles": border_tiles, "lower_tiles": lower_tiles, "inverse_diag": inverse_diag, "owner_map": owner_map}


def pair_slot(later, earlier):
    return later * (later - 1) // 2 + earlier


def pack_rows(rows_here, owners, devices, most):
    onehot = (owners[:, None] == jnp.arange(devices, dtype=jnp.int32)[None, :]).astype(jnp.int32)
    ranks = jnp.cumsum(onehot, axis=0) - onehot
    slots = jnp.sum(ranks * onehot, axis=1)
    target = owners * most + slots
    select = (jnp.arange(devices * most, dtype=jnp.int32)[:, None] == target[None, :]).astype(jnp.float32)
    return jnp.dot(select, rows_here, precision=lax.Precision.HIGHEST, preferred_element_type=jnp.float32)


def reference(pivot_rhs, bound_sol, border_tiles, lower_tiles, inverse_diag, owner_map):
    border_term = lax.dot_general(border_tiles, bound_sol, (((0,), (0,)), ((), ())), preferred_element_type=jnp.float32)
    solved = [None] * NB
    rounded = [None] * NB
    for k in reversed(range(NB)):
        total = border_term[k]
        for j in range(k + 1, NB):
            total = total + lax.dot_general(lower_tiles[pair_slot(j, k)], rounded[j], (((0,), (0,)), ((), ())), preferred_element_type=jnp.float32)
        residual = (pivot_rhs[k] - total).astype(jnp.bfloat16)
        solved[k] = lax.dot_general(inverse_diag[k], residual, (((0,), (0,)), ((), ())), preferred_element_type=jnp.float32)
        rounded[k] = solved[k].astype(jnp.bfloat16)
    solution = jnp.stack(solved)
    per_block = BS // DEVICES
    by_sender = solution.reshape(NB, DEVICES, per_block, NRHS).transpose(1, 0, 2, 3).reshape(DEVICES, ROWS_DEV, NRHS)
    owners = owner_map[:, :, 0]

    def packer(pair):
        return pack_rows(pair[0], pair[1], DEVICES, MOST)

    buffers = lax.map(packer, (by_sender, owners))
    buffers = buffers.reshape(DEVICES, DEVICES, MOST, NRHS).transpose(1, 0, 2, 3)
    return buffers.reshape(DEVICES * DEVICES * MOST, NRHS)
```

```python
import functools

import jax
import jax.numpy as jnp
from jax import lax
from jax.experimental import pallas as pl
from jax.experimental.pallas import tpu as pltpu
from jax.sharding import PartitionSpec as P

MESH = pl.DeviceIdType.MESH
MID_LAGS = (0, 3, 6, 9, 11, 14)
END_LAGS = (0, 0, 8, 10, 12, 14)
LAG_BASE = 15
GROUP = 4


def solve_kernel(dims, pend_in, lower_in, inv_in, out, pend, lower, inv, xt, part, qbuf, sbuf, recv_a, xbuf, resid,
                 pair_s, pair_r, rs_s, rs_r, s_sem, a_sem, x_sem, b_sem, bs_sem, ps_sem, pr_sem,
                 rss_sem, rsr_sem, ags_sem, agr_sem, fs_sem, fr_sem, o_sem, pl_sem, il_sem, ll_sem):
    R, C, NB, N, PC = dims
    M = C // 2
    HALF = N // 2
    depth = inv.shape[2]
    by_lanes = N // C < 16
    CH = HALF if by_lanes else HALF // M
    LW = depth // M if by_lanes else depth
    S = 2 * PC
    items = NB * PC
    z = lax.axis_index("rows")
    c = lax.axis_index("cols")
    h = lax.rem(c, 2)
    m = c // 2
    low = z < R // 2
    mid = jnp.logical_or(z == R // 2 - 1, z == R // 2)
    edge = jnp.logical_or(z == 0, z == R - 1)
    inner = jnp.where(low, z + 1, z - 1)
    outer = jnp.where(low, z - 1, z + 1)
    outer_safe = jnp.where(edge, inner, outer)
    partner = c + 1 - 2 * h

    def peer(d):
        return 2 * lax.rem(m + d, M) + h

    def share(base, q):
        if by_lanes:
            return pl.ds(pl.multiple_of(base, HALF), HALF), pl.ds(pl.multiple_of(q * LW, LW), LW)
        return pl.ds(pl.multiple_of(base + q * CH, CH), CH), slice(None)

    def load_pend(k):
        return pltpu.make_async_copy(pend_in.at[k], pend.at[k], pl_sem.at[k])

    def load_inv(k):
        return pltpu.make_async_copy(inv_in.at[k], inv.at[k], il_sem.at[k])

    load_lower = pltpu.make_async_copy(lower_in, lower, ll_sem)
    load_pend(NB - 1).start()
    load_inv(NB - 1).start()
    load_lower.start()
    for k in range(NB - 2, -1, -1):
        load_pend(k).start()
        load_inv(k).start()

    barrier = pltpu.get_barrier_semaphore()

    @pl.when(z > 0)
    def _():
        pl.semaphore_signal(barrier, inc=1, device_id={"rows": z - 1}, device_id_type=MESH)

    @pl.when(z < R - 1)
    def _():
        pl.semaphore_signal(barrier, inc=1, device_id={"rows": z + 1}, device_id_type=MESH)

    pl.semaphore_signal(barrier, inc=1, device_id={"cols": partner}, device_id_type=MESH)
    for d in range(1, M):
        pl.semaphore_signal(barrier, inc=1, device_id={"cols": peer(d)}, device_id_type=MESH)
    pl.semaphore_wait(barrier, M + jnp.where(edge, 1, 2))

    def remote(src, dst, ss, rs, where):
        return pltpu.make_async_remote_copy(src_ref=src, dst_ref=dst, send_sem=ss, recv_sem=rs,
                                            device_id=where, device_id_type=MESH)

    def inner_copy(s):
        return remote(sbuf.at[s], recv_a.at[s], s_sem.at[s], a_sem.at[s], {"rows": inner})

    def swap_copy(s):
        return remote(sbuf.at[s], xbuf.at[s], s_sem.at[s], x_sem.at[s], {"rows": inner})

    def back_copy(s):
        return remote(resid.at[s], resid.at[s], bs_sem.at[s], b_sem.at[s], {"rows": outer_safe})

    def pair_copy(s):
        return remote(pair_s.at[s], pair_r.at[s], ps_sem.at[s], pr_sem.at[s], {"cols": partner})

    def rs_copy(s, d):
        rows, lanes = share(0, lax.rem(m + d, M))
        return remote(rs_s.at[s, rows, lanes], rs_r.at[s, d - 1], rss_sem.at[s, d - 1], rsr_sem.at[s, d - 1],
                      {"cols": peer(d)})

    def ag_copy(s, k, p, d):
        rows, lanes = share(p * N + h * HALF, m)
        return remote(xt.at[k, rows, lanes], xt.at[k, rows, lanes], ags_sem.at[s, d - 1], agr_sem.at[s, d - 1],
                      {"cols": peer(d)})

    def fwd_copy(s, k, p):
        rows = pl.ds(pl.multiple_of(p * N + h * HALF, HALF), HALF)
        return remote(xt.at[k, rows], xt.at[k, rows], fs_sem.at[s], fr_sem.at[s], {"cols": partner})

    def split(i):
        k = NB - 1 - i // PC
        return k, lax.rem(i, PC), lax.rem(i, S)

    def piece(p):
        return pl.ds(pl.multiple_of(p * N, N), N)

    def first(i):
        k, p, s = split(i)

        @pl.when(i >= PC)
        def _():
            kb, pb, sb = split(i - PC)
            fwd_copy(sb, kb, pb).wait_recv()

        @pl.when(p == 0)
        def _():
            load_pend(k).wait()

        @pl.when(i == PC)
        def _():
            load_lower.wait()

        part[p] = pend[k, piece(p), :]

        def add(j, carry):
            part[p] += jnp.dot(xt[j, piece(p), :], lower[j * (j - 1) // 2 + k],
                               preferred_element_type=jnp.float32)
            return carry

        lax.fori_loop(k + 1, NB, add, 0)

        @pl.when(edge)
        def _():
            sbuf[s] = part[p].astype(jnp.bfloat16)
            inner_copy(s).start()

    def second(i):
        k, p, s = split(i)

        @pl.when(jnp.logical_not(edge))
        def _():
            inner_copy(s).wait_recv()
            part[p] += recv_a[s].astype(jnp.float32)
            sbuf[s] = part[p].astype(jnp.bfloat16)

            @pl.when(mid)
            def _():
                swap_copy(s).start()

            @pl.when(jnp.logical_not(mid))
            def _():
                inner_copy(s).start()

    def third(i):
        k, p, s = split(i)

        @pl.when(mid)
        def _():
            swap_copy(s).wait_recv()
            resid[s] = (-(part[p] + xbuf[s].astype(jnp.float32))).astype(jnp.bfloat16)

        @pl.when(jnp.logical_not(mid))
        def _():
            back_copy(s).wait_recv()

        @pl.when(jnp.logical_not(edge))
        def _():
            back_copy(s).start()

        @pl.when(p == 0)
        def _():
            load_inv(k).wait()

        qbuf[p] = jnp.dot(resid[s], inv[k], preferred_element_type=jnp.float32)
        theirs = pl.ds(pl.multiple_of((1 - h) * HALF, HALF), HALF)
        pair_s[s] = qbuf[p, theirs, :].astype(jnp.bfloat16)
        pair_copy(s).start()

    def fourth(i):
        k, p, s = split(i)
        pair_copy(s).wait_recv()
        mine = pl.ds(pl.multiple_of(h * HALF, HALF), HALF)
        both = qbuf[p, mine, :] + pair_r[s].astype(jnp.float32)
        qbuf[p, mine, :] = both
        rs_s[s] = both.astype(jnp.bfloat16)
        for d in range(1, M):
            rs_copy(s, d).start()

    def fifth(i):
        k, p, s = split(i)
        rows, lanes = share(h * HALF, m)
        total = qbuf[p, rows, lanes]
        for d in range(1, M):
            rs_copy(s, d).wait_recv()
        for d in range(1, M):
            total = total + rs_r[s, d - 1].astype(jnp.float32)
        rows, lanes = share(p * N + h * HALF, m)
        xt[k, rows, lanes] = total.astype(jnp.bfloat16)
        for d in range(1, M):
            ag_copy(s, k, p, d).start()

    def sixth(i):
        k, p, s = split(i)
        for d in range(1, M):
            ag_copy(s, k, p, d).wait_recv()
        fwd_copy(s, k, p).start()

    def sends(i):
        k, p, s = split(i)
        inner_copy(s).wait_send()

        @pl.when(jnp.logical_not(edge))
        def _():
            back_copy(s).wait_send()

        pair_copy(s).wait_send()
        for d in range(1, M):
            rs_copy(s, d).wait_send()
        for d in range(1, M):
            ag_copy(s, k, p, d).wait_send()
        fwd_copy(s, k, p).wait_send()

    mid_lags = [min(lag, LAG_BASE) * (PC - 1) // LAG_BASE for lag in MID_LAGS]
    end_lags = [min(lag, LAG_BASE) * (PC - 1) // LAG_BASE for lag in END_LAGS]
    stages = list(zip((first, second, third, fourth, fifth, sixth), mid_lags, end_lags))
    stages.append((sends, PC + PC // 2, PC + PC // 2))

    def step(t, carry):
        for stage, mid_lag, end_lag in stages:
            i = t - jnp.where(mid, mid_lag, end_lag)

            @pl.when(jnp.logical_and(i >= 0, i < items))
            def _(stage=stage, i=i):
                stage(i)
        return carry

    lax.fori_loop(0, items + PC + PC // 2, step, 0)

    def last(i, carry):
        k, p, s = split(i)
        fwd_copy(s, k, p).wait_recv()
        return carry

    lax.fori_loop(items - PC, items, last, 0)
    cut = out.shape[2]
    source = xt
    if cut < depth:
        source = xt.at[:, :, pl.ds(pl.multiple_of(c * cut, cut), cut)]
    write = pltpu.make_async_copy(source, out, o_sem)
    write.start()
    write.wait()


def solve(pend, lower, inv, R, C):
    NB, sources, width = pend.shape
    depth = inv.shape[2]
    wide = depth % (64 * C) == 0
    N = min(8 * C if wide else 16 * C, sources // 2)
    PC = sources // N
    S = 2 * PC
    M = C // 2
    bf, f32 = jnp.bfloat16, jnp.float32
    dma = pltpu.SemaphoreType.DMA
    anywhere = pl.BlockSpec(memory_space=pl.ANY)
    cut = depth // C if depth % (128 * C) == 0 else depth
    return pl.pallas_call(
        functools.partial(solve_kernel, (R, C, NB, N, PC)),
        out_shape=jax.ShapeDtypeStruct((NB, sources, cut), bf),
        in_specs=[anywhere, anywhere, anywhere],
        out_specs=pl.BlockSpec(memory_space=pl.ANY),
        scratch_shapes=[
            pltpu.VMEM(pend.shape, f32),
            pltpu.VMEM(lower.shape, bf),
            pltpu.VMEM(inv.shape, bf),
            pltpu.VMEM((NB, sources, depth), bf),
            pltpu.VMEM((PC, N, width), f32),
            pltpu.VMEM((PC, N, depth), f32),
            pltpu.VMEM((S, N, width), bf),
            pltpu.VMEM((S, N, width), bf),
            pltpu.VMEM((S, N, width), bf),
            pltpu.VMEM((S, N, width), bf),
            pltpu.VMEM((S, N // 2, depth), bf),
            pltpu.VMEM((S, N // 2, depth), bf),
            pltpu.VMEM((S, N // 2, depth), bf),
            pltpu.VMEM((S, M - 1) + ((N // 2, depth // M) if N // C < 16 else (N // C, depth)), bf),
            dma((S,)), dma((S,)), dma((S,)), dma((S,)), dma((S,)), dma((S,)), dma((S,)),
            dma((S, M - 1)), dma((S, M - 1)), dma((S, M - 1)), dma((S, M - 1)),
            dma((S,)), dma((S,)), dma, dma((NB,)), dma((NB,)), dma,
        ],
        compiler_params=pltpu.CompilerParams(
            collective_id=0, has_side_effects=True, vmem_limit_bytes=60 * 1024 * 1024
        ),
    )(pend, lower, inv)


def fused_kernel(dims, pend_in, lower_in, inv_in, target, out, pend, lower, inv, xt, part, qbuf, sbuf, recv_a, xbuf, resid,
                 pair_s, pair_r, rs_s, rs_r, s_sem, a_sem, x_sem, b_sem, bs_sem, ps_sem, pr_sem,
                 rss_sem, rsr_sem, ags_sem, agr_sem, fs_sem, fr_sem, o_sem, pl_sem, il_sem, ll_sem,
                 select, own, pack, recv, ks_sem, kr_sem):
    R, C, NB, N, PC, most = dims
    devices = R * C
    M = C // 2
    HALF = N // 2
    depth = inv.shape[2]
    LW = depth // M
    LB = depth // C
    G, slots, GW = pack.shape
    PG = GW // N
    S = 2 * PC
    items = NB * PC
    z = lax.axis_index("rows")
    c = lax.axis_index("cols")
    h = lax.rem(c, 2)
    m = c // 2
    low = z < R // 2
    mid = jnp.logical_or(z == R // 2 - 1, z == R // 2)
    edge = jnp.logical_or(z == 0, z == R - 1)
    inner = jnp.where(low, z + 1, z - 1)
    outer = jnp.where(low, z - 1, z + 1)
    outer_safe = jnp.where(edge, inner, outer)
    partner = c + 1 - 2 * h
    me = z * C + c

    def peer(d):
        return 2 * lax.rem(m + d, M) + h

    def share(base, q):
        return pl.ds(pl.multiple_of(base, HALF), HALF), pl.ds(pl.multiple_of(q * LW, LW), LW)

    def load_pend(k):
        return pltpu.make_async_copy(pend_in.at[k], pend.at[k], pl_sem.at[k])

    def load_inv(k):
        return pltpu.make_async_copy(inv_in.at[k], inv.at[k], il_sem.at[k])

    load_lower = pltpu.make_async_copy(lower_in, lower, ll_sem)
    load_pend(NB - 1).start()
    load_inv(NB - 1).start()
    load_lower.start()
    for k in range(NB - 2, -1, -1):
        load_pend(k).start()
        load_inv(k).start()

    barrier = pltpu.get_barrier_semaphore()

    def device(d):
        o = lax.rem(me + d, devices)
        return o, {"rows": o // C, "cols": lax.rem(o, C)}

    def greet(d, carry):
        pl.semaphore_signal(barrier, inc=1, device_id=device(d)[1], device_id_type=MESH)
        return carry

    lax.fori_loop(1, devices, greet, 0)
    RC = 128

    def choose(q, carry):
        rows = pl.ds(pl.multiple_of(q * RC, RC), RC)
        ids = q * RC + lax.broadcasted_iota(jnp.int32, (RC, select.shape[1]), 0)
        select[rows, :] = jnp.where(ids == target[...], 1.0, 0.0).astype(jnp.bfloat16)
        return carry

    lax.fori_loop(0, slots // RC, choose, 0)
    pl.semaphore_wait(barrier, devices - 1)

    def remote(src, dst, ss, rs, where):
        return pltpu.make_async_remote_copy(src_ref=src, dst_ref=dst, send_sem=ss, recv_sem=rs,
                                            device_id=where, device_id_type=MESH)

    def inner_copy(s):
        return remote(sbuf.at[s], recv_a.at[s], s_sem.at[s], a_sem.at[s], {"rows": inner})

    def swap_copy(s):
        return remote(sbuf.at[s], xbuf.at[s], s_sem.at[s], x_sem.at[s], {"rows": inner})

    def back_copy(s):
        return remote(resid.at[s], resid.at[s], bs_sem.at[s], b_sem.at[s], {"rows": outer_safe})

    def pair_copy(s):
        return remote(pair_s.at[s], pair_r.at[s], ps_sem.at[s], pr_sem.at[s], {"cols": partner})

    def rs_copy(s, d):
        rows, lanes = share(0, lax.rem(m + d, M))
        return remote(rs_s.at[s, rows, lanes], rs_r.at[s, d - 1], rss_sem.at[s, d - 1], rsr_sem.at[s, d - 1],
                      {"cols": peer(d)})

    def ag_copy(s, k, p, d):
        rows, lanes = share(p * N + h * HALF, m)
        return remote(xt.at[k, rows, lanes], xt.at[k, rows, lanes], ags_sem.at[s, d - 1], agr_sem.at[s, d - 1],
                      {"cols": peer(d)})

    def fwd_copy(s, k, p):
        rows = pl.ds(pl.multiple_of(p * N + h * HALF, HALF), HALF)
        return remote(xt.at[k, rows], xt.at[k, rows], fs_sem.at[s], fr_sem.at[s], {"cols": partner})

    def half_copy(s, p):
        rows = pl.ds(pl.multiple_of(p * N + h * HALF, HALF), HALF)
        lanes = pl.ds(pl.multiple_of(partner * LB, LB), LB)
        return remote(xt.at[0, rows, lanes], xt.at[0, rows, lanes], fs_sem.at[s], fr_sem.at[s], {"cols": partner})

    def section(rows):
        return pl.ds(pl.multiple_of(rows * most, most), most)

    def send_copy(g, d):
        o, where = device(d)
        return remote(pack.at[g, section(o)], recv.at[g, section(me)], ks_sem.at[g], kr_sem.at[g], where)

    def out_copy(g):
        return pltpu.make_async_copy(recv.at[g], out.at[:, pl.ds(pl.multiple_of(g * GW, GW), GW)], o_sem.at[g])

    def split(i):
        k = NB - 1 - i // PC
        return k, lax.rem(i, PC), lax.rem(i, S)

    def piece(p):
        return pl.ds(pl.multiple_of(p * N, N), N)

    def first(i):
        k, p, s = split(i)

        @pl.when(i >= PC)
        def _():
            kb, pb, sb = split(i - PC)
            fwd_copy(sb, kb, pb).wait_recv()

        @pl.when(p == 0)
        def _():
            load_pend(k).wait()

        @pl.when(i == PC)
        def _():
            load_lower.wait()

        part[p] = pend[k, piece(p), :]

        def add(j, carry):
            part[p] += jnp.dot(xt[j, piece(p), :], lower[j * (j - 1) // 2 + k],
                               preferred_element_type=jnp.float32)
            return carry

        lax.fori_loop(k + 1, NB, add, 0)

        @pl.when(edge)
        def _():
            sbuf[s] = part[p].astype(jnp.bfloat16)
            inner_copy(s).start()

    def second(i):
        k, p, s = split(i)

        @pl.when(jnp.logical_not(edge))
        def _():
            inner_copy(s).wait_recv()
            part[p] += recv_a[s].astype(jnp.float32)
            sbuf[s] = part[p].astype(jnp.bfloat16)

            @pl.when(mid)
            def _():
                swap_copy(s).start()

            @pl.when(jnp.logical_not(mid))
            def _():
                inner_copy(s).start()

    def third(i):
        k, p, s = split(i)

        @pl.when(mid)
        def _():
            swap_copy(s).wait_recv()
            resid[s] = (-(part[p] + xbuf[s].astype(jnp.float32))).astype(jnp.bfloat16)

        @pl.when(jnp.logical_not(mid))
        def _():
            back_copy(s).wait_recv()

        @pl.when(jnp.logical_not(edge))
        def _():
            back_copy(s).start()

        @pl.when(p == 0)
        def _():
            load_inv(k).wait()

        qbuf[p] = jnp.dot(resid[s], inv[k], preferred_element_type=jnp.float32)
        theirs = pl.ds(pl.multiple_of((1 - h) * HALF, HALF), HALF)
        pair_s[s] = qbuf[p, theirs, :].astype(jnp.bfloat16)
        pair_copy(s).start()

    def fourth(i):
        k, p, s = split(i)
        pair_copy(s).wait_recv()
        mine = pl.ds(pl.multiple_of(h * HALF, HALF), HALF)
        both = qbuf[p, mine, :] + pair_r[s].astype(jnp.float32)
        qbuf[p, mine, :] = both
        rs_s[s] = both.astype(jnp.bfloat16)
        for d in range(1, M):
            rs_copy(s, d).start()

    def fifth(i):
        k, p, s = split(i)
        rows, lanes = share(h * HALF, m)
        total = qbuf[p, rows, lanes]
        for d in range(1, M):
            rs_copy(s, d).wait_recv()
        for d in range(1, M):
            total = total + rs_r[s, d - 1].astype(jnp.float32)
        rows, lanes = share(p * N + h * HALF, m)
        xt[k, rows, lanes] = total.astype(jnp.bfloat16)

        @pl.when(k > 0)
        def _():
            for d in range(1, M):
                ag_copy(s, k, p, d).start()

        @pl.when(k == 0)
        def _():
            half_copy(s, p).start()

    def sixth(i):
        k, p, s = split(i)

        @pl.when(k > 0)
        def _():
            for d in range(1, M):
                ag_copy(s, k, p, d).wait_recv()
            fwd_copy(s, k, p).start()

    def seventh(i):
        k, p, s = split(i)

        @pl.when(k == 0)
        def _():
            half_copy(s, p).wait_recv()

        @pl.when(jnp.logical_and(k == 0, lax.rem(p, PG) == PG - 1))
        def _():
            g = p // PG
            rows = pl.ds(pl.multiple_of(g * GW, GW), GW)
            lanes = pl.ds(pl.multiple_of(c * LB, LB), LB)
            for b in range(NB):
                own[:, b * LB:(b + 1) * LB] = xt[b, rows, lanes]

            def fill(q, carry):
                part_rows = pl.ds(pl.multiple_of(q * RC, RC), RC)
                pack[g, part_rows, :] = lax.dot_general(
                    select[part_rows, :], own[...], (((1,), (1,)), ((), ())), preferred_element_type=jnp.float32
                ).astype(jnp.bfloat16)
                return carry

            lax.fori_loop(0, slots // RC, fill, 0)

            def send(d, carry):
                send_copy(g, d).start()
                return carry

            lax.fori_loop(1, devices, send, 0)
            pltpu.make_async_copy(pack.at[g, section(me)], recv.at[g, section(me)], kr_sem.at[g]).start()

    def sends(i):
        k, p, s = split(i)
        inner_copy(s).wait_send()

        @pl.when(jnp.logical_not(edge))
        def _():
            back_copy(s).wait_send()

        pair_copy(s).wait_send()
        for d in range(1, M):
            rs_copy(s, d).wait_send()

        @pl.when(k > 0)
        def _():
            for d in range(1, M):
                ag_copy(s, k, p, d).wait_send()
            fwd_copy(s, k, p).wait_send()

        @pl.when(k == 0)
        def _():
            half_copy(s, p).wait_send()

    mid_lags = [min(lag, LAG_BASE) * (PC - 1) // LAG_BASE for lag in MID_LAGS]
    end_lags = [min(lag, LAG_BASE) * (PC - 1) // LAG_BASE for lag in END_LAGS]
    stages = list(zip((first, second, third, fourth, fifth, sixth), mid_lags, end_lags))
    stages.append((seventh, PC - 1, PC - 1))
    stages.append((sends, PC + PC // 2, PC + PC // 2))

    def step(t, carry):
        for stage, mid_lag, end_lag in stages:
            i = t - jnp.where(mid, mid_lag, end_lag)

            @pl.when(jnp.logical_and(i >= 0, i < items))
            def _(stage=stage, i=i):
                stage(i)
        return carry

    lax.fori_loop(0, items + PC + PC // 2, step, 0)

    def arrive(g, carry):
        pltpu.make_async_copy(recv.at[g], recv.at[g], kr_sem.at[g]).wait()
        out_copy(g).start()
        return carry

    lax.fori_loop(0, G, arrive, 0)

    def finish(g, carry):
        sent = pack.at[g, pl.ds(0, slots - most)]
        pltpu.make_async_copy(sent, sent, ks_sem.at[g]).wait()
        out_copy(g).wait()
        return carry

    lax.fori_loop(0, G, finish, 0)


def fused(pend, lower, inv, target, R, C, most):
    NB, sources, width = pend.shape
    depth = inv.shape[2]
    devices = R * C
    N = 8 * C
    PC = sources // N
    S = 2 * PC
    M = C // 2
    GW = GROUP * N
    G = sources // GW
    bf, f32 = jnp.bfloat16, jnp.float32
    dma = pltpu.SemaphoreType.DMA
    anywhere = pl.BlockSpec(memory_space=pl.ANY)
    return pl.pallas_call(
        functools.partial(fused_kernel, (R, C, NB, N, PC, most)),
        out_shape=jax.ShapeDtypeStruct((devices * most, sources), bf),
        in_specs=[anywhere, anywhere, anywhere, pl.BlockSpec(memory_space=pltpu.VMEM)],
        out_specs=pl.BlockSpec(memory_space=pl.ANY),
        scratch_shapes=[
            pltpu.VMEM(pend.shape, f32),
            pltpu.VMEM(lower.shape, bf),
            pltpu.VMEM(inv.shape, bf),
            pltpu.VMEM((NB, sources, depth), bf),
            pltpu.VMEM((PC, N, width), f32),
            pltpu.VMEM((PC, N, depth), f32),
            pltpu.VMEM((S, N, width), bf),
            pltpu.VMEM((S, N, width), bf),
            pltpu.VMEM((S, N, width), bf),
            pltpu.VMEM((S, N, width), bf),
            pltpu.VMEM((S, N // 2, depth), bf),
            pltpu.VMEM((S, N // 2, depth), bf),
            pltpu.VMEM((S, N // 2, depth), bf),
            pltpu.VMEM((S, M - 1, N // 2, depth // M), bf),
            dma((S,)), dma((S,)), dma((S,)), dma((S,)), dma((S,)), dma((S,)), dma((S,)),
            dma((S, M - 1)), dma((S, M - 1)), dma((S, M - 1)), dma((S, M - 1)),
            dma((S,)), dma((S,)), dma((G,)), dma((NB,)), dma((NB,)), dma,
            pltpu.VMEM((devices * most, target.shape[1]), bf),
            pltpu.VMEM((GW, target.shape[1]), bf),
            pltpu.VMEM((G, devices * most, GW), bf),
            pltpu.VMEM((G, devices * most, GW), bf),
            dma((G,)), dma((G,)),
        ],
        compiler_params=pltpu.CompilerParams(
            collective_id=1, has_side_effects=True, vmem_limit_bytes=60 * 1024 * 1024
        ),
    )(pend, lower, inv, target)


def local(pivot_rhs, bound_sol, border_tiles, lower_tiles, inverse_diag, owner_map):
    R = lax.axis_size("rows")
    C = lax.axis_size("cols")
    devices = R * C
    blocks, _, sources = pivot_rhs.shape
    rows_dev = owner_map.shape[1]
    per_block = rows_dev // blocks
    most = max(2, 2 * rows_dev // devices)
    border = lax.dot_general(
        bound_sol, border_tiles, (((0,), (0,)), ((), ())), preferred_element_type=jnp.float32
    )
    row = lax.axis_index("rows")
    if R % blocks == 0:
        block = row // (R // blocks)
        mine = jnp.logical_and(jnp.arange(blocks) == block, lax.rem(row, R // blocks) == 0)
        rhs = lax.dynamic_index_in_dim(pivot_rhs, block, 0, keepdims=False).T[None]
        rhs = jnp.where(mine[:, None, None], rhs, 0.0)
    else:
        rhs = jnp.where(row == R // 2 - 1, pivot_rhs.transpose(0, 2, 1), 0.0)
    pend = border.transpose(1, 0, 2) - rhs
    owners = owner_map[0, :, 0]
    onehot = (owners[:, None] == jnp.arange(devices, dtype=jnp.int32)[None, :]).astype(jnp.int32)
    ranks = jnp.cumsum(onehot, axis=0) - onehot
    slots = jnp.sum(ranks * onehot, axis=1)
    target = owners * most + slots
    pieces = 8 * C
    if pieces // C < 16 and per_block % 128 == 0 and most % 32 == 0 and sources % (GROUP * pieces) == 0:
        received = fused(pend, lower_tiles, inverse_diag, target[None, :], R, C, most)
        return received.astype(jnp.float32)
    xt = solve(pend, lower_tiles, inverse_diag, R, C)

    own = xt
    if xt.shape[2] > per_block:
        own = lax.dynamic_slice_in_dim(xt, lax.axis_index("cols") * per_block, per_block, axis=2)
    select = (jnp.arange(devices * most, dtype=jnp.int32)[:, None] == target[None, :]).astype(jnp.bfloat16)
    select = select.reshape(devices * most, blocks, per_block)
    packed = lax.dot_general(
        select, own, (((1, 2), (0, 2)), ((), ())), preferred_element_type=jnp.float32
    ).astype(jnp.bfloat16)
    received = lax.all_to_all(
        packed.reshape(devices, most, sources), ("rows", "cols"), split_axis=0, concat_axis=0, tiled=True
    )
    return received.reshape(devices * most, sources).astype(jnp.float32)


def solution(mesh):
    placed = (
        P(None, "cols", None),
        P("rows", None),
        P("rows", None, "cols"),
        P(None, "rows", "cols"),
        P(None, "cols", "rows"),
        P(("rows", "cols"), None, None),
    )
    return jax.shard_map(
        local, mesh=mesh, in_specs=placed, out_specs=P(("rows", "cols"), None), check_vma=False
    )
```

```python
import functools

import jax
import jax.numpy as jnp
from jax import lax
from jax.experimental import pallas as pl
from jax.experimental.pallas import tpu as pltpu
from jax.sharding import PartitionSpec as P

MESH = pl.DeviceIdType.MESH
MID_LAGS = (0, 3, 6, 8, 11, 14)
END_LAGS = (0, 0, 9, 10, 12, 14)
LAG_BASE = 15
GROUP = 4
RAW = 6
RAW_ROWS = 256
VMEM_BYTES = 63 * 1024 * 1024 + 512 * 1024


def solve_kernel(dims, pend_in, lower_in, inv_in, out, pend, lower, inv, xt, part, qbuf, sbuf, recv_a, xbuf, resid,
                 pair_s, pair_r, rs_s, rs_r, s_sem, a_sem, x_sem, b_sem, bs_sem, ps_sem, pr_sem,
                 rss_sem, rsr_sem, ags_sem, agr_sem, fs_sem, fr_sem, o_sem, pl_sem, il_sem, ll_sem):
    R, C, NB, N, PC = dims
    M = C // 2
    HALF = N // 2
    depth = inv.shape[2]
    by_lanes = N // C < 16
    CH = HALF if by_lanes else HALF // M
    LW = depth // M if by_lanes else depth
    S = 2 * PC
    items = NB * PC
    z = lax.axis_index("rows")
    c = lax.axis_index("cols")
    h = lax.rem(c, 2)
    m = c // 2
    low = z < R // 2
    mid = jnp.logical_or(z == R // 2 - 1, z == R // 2)
    edge = jnp.logical_or(z == 0, z == R - 1)
    inner = jnp.where(low, z + 1, z - 1)
    outer = jnp.where(low, z - 1, z + 1)
    outer_safe = jnp.where(edge, inner, outer)
    partner = c + 1 - 2 * h

    def peer(d):
        return 2 * lax.rem(m + d, M) + h

    def share(base, q):
        if by_lanes:
            return pl.ds(pl.multiple_of(base, HALF), HALF), pl.ds(pl.multiple_of(q * LW, LW), LW)
        return pl.ds(pl.multiple_of(base + q * CH, CH), CH), slice(None)

    def load_pend(k):
        return pltpu.make_async_copy(pend_in.at[k], pend.at[k], pl_sem.at[k])

    def load_inv(k):
        return pltpu.make_async_copy(inv_in.at[k], inv.at[k], il_sem.at[k])

    load_lower = pltpu.make_async_copy(lower_in, lower, ll_sem)
    load_pend(NB - 1).start()
    load_inv(NB - 1).start()
    load_lower.start()
    for k in range(NB - 2, -1, -1):
        load_pend(k).start()
        load_inv(k).start()

    barrier = pltpu.get_barrier_semaphore()

    @pl.when(z > 0)
    def _():
        pl.semaphore_signal(barrier, inc=1, device_id={"rows": z - 1}, device_id_type=MESH)

    @pl.when(z < R - 1)
    def _():
        pl.semaphore_signal(barrier, inc=1, device_id={"rows": z + 1}, device_id_type=MESH)

    pl.semaphore_signal(barrier, inc=1, device_id={"cols": partner}, device_id_type=MESH)
    for d in range(1, M):
        pl.semaphore_signal(barrier, inc=1, device_id={"cols": peer(d)}, device_id_type=MESH)
    pl.semaphore_wait(barrier, M + jnp.where(edge, 1, 2))

    def remote(src, dst, ss, rs, where):
        return pltpu.make_async_remote_copy(src_ref=src, dst_ref=dst, send_sem=ss, recv_sem=rs,
                                            device_id=where, device_id_type=MESH)

    def inner_copy(s):
        return remote(sbuf.at[s], recv_a.at[s], s_sem.at[s], a_sem.at[s], {"rows": inner})

    def swap_copy(s):
        return remote(sbuf.at[s], xbuf.at[s], s_sem.at[s], x_sem.at[s], {"rows": inner})

    def back_copy(s):
        return remote(resid.at[s], resid.at[s], bs_sem.at[s], b_sem.at[s], {"rows": outer_safe})

    def pair_copy(s):
        return remote(pair_s.at[s], pair_r.at[s], ps_sem.at[s], pr_sem.at[s], {"cols": partner})

    def rs_copy(s, d):
        rows, lanes = share(0, lax.rem(m + d, M))
        return remote(rs_s.at[s, rows, lanes], rs_r.at[s, d - 1], rss_sem.at[s, d - 1], rsr_sem.at[s, d - 1],
                      {"cols": peer(d)})

    def ag_copy(s, k, p, d):
        rows, lanes = share(p * N + h * HALF, m)
        return remote(xt.at[k, rows, lanes], xt.at[k, rows, lanes], ags_sem.at[s, d - 1], agr_sem.at[s, d - 1],
                      {"cols": peer(d)})

    def fwd_copy(s, k, p):
        rows = pl.ds(pl.multiple_of(p * N + h * HALF, HALF), HALF)
        return remote(xt.at[k, rows], xt.at[k, rows], fs_sem.at[s], fr_sem.at[s], {"cols": partner})

    def split(i):
        k = NB - 1 - i // PC
        return k, lax.rem(i, PC), lax.rem(i, S)

    def piece(p):
        return pl.ds(pl.multiple_of(p * N, N), N)

    def first(i):
        k, p, s = split(i)

        @pl.when(i >= PC)
        def _():
            kb, pb, sb = split(i - PC)
            fwd_copy(sb, kb, pb).wait_recv()

        @pl.when(p == 0)
        def _():
            load_pend(k).wait()

        @pl.when(i == PC)
        def _():
            load_lower.wait()

        part[p] = pend[k, piece(p), :]

        def add(j, carry):
            part[p] += jnp.dot(xt[j, piece(p), :], lower[j * (j - 1) // 2 + k],
                               preferred_element_type=jnp.float32)
            return carry

        lax.fori_loop(k + 1, NB, add, 0)

        @pl.when(edge)
        def _():
            sbuf[s] = part[p].astype(jnp.bfloat16)
            inner_copy(s).start()

    def second(i):
        k, p, s = split(i)

        @pl.when(jnp.logical_not(edge))
        def _():
            inner_copy(s).wait_recv()
            part[p] += recv_a[s].astype(jnp.float32)
            sbuf[s] = part[p].astype(jnp.bfloat16)

            @pl.when(mid)
            def _():
                swap_copy(s).start()

            @pl.when(jnp.logical_not(mid))
            def _():
                inner_copy(s).start()

    def third(i):
        k, p, s = split(i)

        @pl.when(mid)
        def _():
            swap_copy(s).wait_recv()
            resid[s] = (-(part[p] + xbuf[s].astype(jnp.float32))).astype(jnp.bfloat16)

        @pl.when(jnp.logical_not(mid))
        def _():
            back_copy(s).wait_recv()

        @pl.when(jnp.logical_not(edge))
        def _():
            back_copy(s).start()

        @pl.when(p == 0)
        def _():
            load_inv(k).wait()

        qbuf[p] = jnp.dot(resid[s], inv[k], preferred_element_type=jnp.float32)
        theirs = pl.ds(pl.multiple_of((1 - h) * HALF, HALF), HALF)
        pair_s[s] = qbuf[p, theirs, :].astype(jnp.bfloat16)
        pair_copy(s).start()

    def fourth(i):
        k, p, s = split(i)
        pair_copy(s).wait_recv()
        mine = pl.ds(pl.multiple_of(h * HALF, HALF), HALF)
        both = qbuf[p, mine, :] + pair_r[s].astype(jnp.float32)
        qbuf[p, mine, :] = both
        rs_s[s] = both.astype(jnp.bfloat16)
        for d in range(1, M):
            rs_copy(s, d).start()

    def fifth(i):
        k, p, s = split(i)
        rows, lanes = share(h * HALF, m)
        total = qbuf[p, rows, lanes]
        for d in range(1, M):
            rs_copy(s, d).wait_recv()
        for d in range(1, M):
            total = total + rs_r[s, d - 1].astype(jnp.float32)
        rows, lanes = share(p * N + h * HALF, m)
        xt[k, rows, lanes] = total.astype(jnp.bfloat16)
        for d in range(1, M):
            ag_copy(s, k, p, d).start()

    def sixth(i):
        k, p, s = split(i)
        for d in range(1, M):
            ag_copy(s, k, p, d).wait_recv()
        fwd_copy(s, k, p).start()

    def sends(i):
        k, p, s = split(i)
        inner_copy(s).wait_send()

        @pl.when(jnp.logical_not(edge))
        def _():
            back_copy(s).wait_send()

        pair_copy(s).wait_send()
        for d in range(1, M):
            rs_copy(s, d).wait_send()
        for d in range(1, M):
            ag_copy(s, k, p, d).wait_send()
        fwd_copy(s, k, p).wait_send()

    mid_lags = [min(lag, LAG_BASE) * (PC - 1) // LAG_BASE for lag in MID_LAGS]
    end_lags = [min(lag, LAG_BASE) * (PC - 1) // LAG_BASE for lag in END_LAGS]
    stages = list(zip((first, second, third, fourth, fifth, sixth), mid_lags, end_lags))
    stages.append((sends, PC + PC // 2, PC + PC // 2))

    def step(t, carry):
        for stage, mid_lag, end_lag in stages:
            i = t - jnp.where(mid, mid_lag, end_lag)

            @pl.when(jnp.logical_and(i >= 0, i < items))
            def _(stage=stage, i=i):
                stage(i)
        return carry

    lax.fori_loop(0, items + PC + PC // 2, step, 0)

    def last(i, carry):
        k, p, s = split(i)
        fwd_copy(s, k, p).wait_recv()
        return carry

    lax.fori_loop(items - PC, items, last, 0)
    cut = out.shape[2]
    source = xt
    if cut < depth:
        source = xt.at[:, :, pl.ds(pl.multiple_of(c * cut, cut), cut)]
    write = pltpu.make_async_copy(source, out, o_sem)
    write.start()
    write.wait()


def solve(pend, lower, inv, R, C):
    NB, sources, width = pend.shape
    depth = inv.shape[2]
    wide = depth % (64 * C) == 0
    N = min(8 * C if wide else 16 * C, sources // 2)
    PC = sources // N
    S = 2 * PC
    M = C // 2
    bf, f32 = jnp.bfloat16, jnp.float32
    dma = pltpu.SemaphoreType.DMA
    anywhere = pl.BlockSpec(memory_space=pl.ANY)
    cut = depth // C if depth % (128 * C) == 0 else depth
    return pl.pallas_call(
        functools.partial(solve_kernel, (R, C, NB, N, PC)),
        out_shape=jax.ShapeDtypeStruct((NB, sources, cut), bf),
        in_specs=[anywhere, anywhere, anywhere],
        out_specs=pl.BlockSpec(memory_space=pl.ANY),
        scratch_shapes=[
            pltpu.VMEM(pend.shape, f32),
            pltpu.VMEM(lower.shape, bf),
            pltpu.VMEM(inv.shape, bf),
            pltpu.VMEM((NB, sources, depth), bf),
            pltpu.VMEM((PC, N, width), f32),
            pltpu.VMEM((PC, N, depth), f32),
            pltpu.VMEM((S, N, width), bf),
            pltpu.VMEM((S, N, width), bf),
            pltpu.VMEM((S, N, width), bf),
            pltpu.VMEM((S, N, width), bf),
            pltpu.VMEM((S, N // 2, depth), bf),
            pltpu.VMEM((S, N // 2, depth), bf),
            pltpu.VMEM((S, N // 2, depth), bf),
            pltpu.VMEM((S, M - 1) + ((N // 2, depth // M) if N // C < 16 else (N // C, depth)), bf),
            dma((S,)), dma((S,)), dma((S,)), dma((S,)), dma((S,)), dma((S,)), dma((S,)),
            dma((S, M - 1)), dma((S, M - 1)), dma((S, M - 1)), dma((S, M - 1)),
            dma((S,)), dma((S,)), dma, dma((NB,)), dma((NB,)), dma,
        ],
        compiler_params=pltpu.CompilerParams(
            collective_id=0, has_side_effects=True, vmem_limit_bytes=60 * 1024 * 1024
        ),
    )(pend, lower, inv)


def fused_kernel(dims, rhs_in, bound_in, border_in, lower_in, inv_in, owners, out, tiles, raw, bound, pend, rhs, inv, xt,
                 part, qbuf, sbuf, recv_a, xbuf, resid, pair_s, pair_r, rs_s, rs_r, select, own, pack, recv,
                 s_sem, a_sem, x_sem, b_sem, bs_sem, ps_sem, pr_sem, rss_sem, rsr_sem, ags_sem, agr_sem, fs_sem, fr_sem,
                 o_sem, raw_sem, bd_sem, rhs_sem, il_sem, ll_sem, ks_sem, kr_sem):
    R, C, NB, N, PC, S, most = dims
    devices = R * C
    M = C // 2
    HALF = N // 2
    depth = inv.shape[2]
    LW = depth // M
    LB = depth // C
    G, slots, GW = pack.shape
    PG = GW // N
    PB = part.shape[0]
    QB = qbuf.shape[0]
    NR, RB = raw.shape[:2]
    QK = bound.shape[1] // depth
    BW = pend.shape[1]
    GB = PC // QK
    chunks = NB * GB
    blocks_raw = bound.shape[1] // RB
    late = []
    for earlier in range(NB - 2, -1, -1):
        late += [(later, earlier) for later in range(earlier + 1, NB)]
    late_unit = {}
    for n, (later, earlier) in enumerate(late):
        unit = NB * QK if n == 0 else (NB - 1) * QK + n - 1
        if n > QK:
            unit = NB * QK + n - QK
        late_unit[later * (later - 1) // 2 + earlier] = unit
    items = NB * PC
    z = lax.axis_index("rows")
    c = lax.axis_index("cols")
    h = lax.rem(c, 2)
    m = c // 2
    low = z < R // 2
    mid = jnp.logical_or(z == R // 2 - 1, z == R // 2)
    edge = jnp.logical_or(z == 0, z == R - 1)
    inner = jnp.where(low, z + 1, z - 1)
    outer = jnp.where(low, z - 1, z + 1)
    outer_safe = jnp.where(edge, inner, outer)
    partner = c + 1 - 2 * h
    me = z * C + c

    def peer(d):
        return 2 * lax.rem(m + d, M) + h

    def share(base, q):
        return pl.ds(pl.multiple_of(base, HALF), HALF), pl.ds(pl.multiple_of(q * LW, LW), LW)

    def load_inv(k):
        return pltpu.make_async_copy(inv_in.at[k], inv.at[k], il_sem.at[k])

    def load_lower(n):
        pair = late[n][0] * (late[n][0] - 1) // 2 + late[n][1]
        return pltpu.make_async_copy(lower_in.at[pair], tiles.at[late_unit[pair]], ll_sem.at[n])

    def load_raw(e):
        pair = NB // 2 - 1 - e // blocks_raw
        rows = pl.ds(pl.multiple_of(lax.rem(e, blocks_raw) * RB, RB), RB)
        slot = lax.rem(e, NR)
        return pltpu.make_async_copy(border_in.at[rows, pl.ds(2 * pair, 2), :], raw.at[slot], raw_sem.at[slot])

    def load_bound(q):
        return pltpu.make_async_copy(bound_in.at[pl.ds(q * depth, depth)], xt.at[q], bd_sem.at[q])

    def load_rhs(g):
        lanes = pl.ds(pl.multiple_of(g * BW, BW), BW)
        slot = lax.rem(g, 2)
        return pltpu.make_async_copy(rhs_in.at[z, :, lanes], rhs.at[slot], rhs_sem.at[slot])

    def untangle(e):
        pair = NB // 2 - 1 - e // blocks_raw
        start = lax.rem(e, blocks_raw) * RB
        rows = pl.ds(pl.multiple_of(lax.rem(start, depth), RB), RB)
        load_raw(e).wait()
        both = jnp.swapaxes(raw[lax.rem(e, NR)], 0, 1)
        for b in range(2):
            tiles[(2 * pair + b) * QK + start // depth, rows, :] = both[b]

        @pl.when(e + NR < NB // 2 * blocks_raw)
        def _():
            load_raw(e + NR).start()

    def turn(g, q):
        rows = pl.ds(pl.multiple_of(g * BW, BW), BW)
        lanes = pl.ds(pl.multiple_of(q * depth, depth), depth)
        bound[rows, lanes] = xt[q, :, rows].T

    def border(j, half):
        k = NB - 1 - j // GB
        g = lax.rem(j, GB)
        slot = lax.rem(j, 2)
        rows = pl.ds(pl.multiple_of(g * BW, BW), BW)
        width = pend.shape[2]
        lanes = pl.ds(pl.multiple_of(half * (width // 2), width // 2), width // 2)
        block = tiles[pl.ds(k * QK, QK), :, lanes].reshape(QK * depth, width // 2)
        pend[slot, :, lanes] = jnp.dot(bound[rows, :], block, preferred_element_type=jnp.float32)

        @pl.when(jnp.logical_and(half == 1, k == z))
        def _():
            load_rhs(g).wait()
            pend[slot] -= rhs[lax.rem(g, 2)].T

            @pl.when(g + 2 < GB)
            def _():
                load_rhs(g + 2).start()

    def unit_of(pair):
        unit = late_unit[0]
        for n in range(1, len(late)):
            unit = jnp.where(pair == n, late_unit[n], unit)
        return unit

    def ahead(j, later):
        k = NB - 1 - j // GB
        rows = pl.ds(pl.multiple_of(lax.rem(j, GB) * BW, BW), BW)
        pend[lax.rem(j, 2)] += jnp.dot(
            xt[later, rows, :], tiles[unit_of(later * (later - 1) // 2 + k)], preferred_element_type=jnp.float32
        )

    def first_raw(e, carry):
        load_raw(e).start()
        return carry

    lax.fori_loop(0, NR, first_raw, 0)
    for q in range(QK - 1, -1, -1):
        load_bound(q).start()
    load_rhs(0).start()
    load_rhs(1).start()
    load_inv(NB - 1).start()

    barrier = pltpu.get_barrier_semaphore()

    def device(d):
        o = lax.rem(me + d, devices)
        return o, {"rows": o // C, "cols": lax.rem(o, C)}

    def greet(d, carry):
        pl.semaphore_signal(barrier, inc=1, device_id=device(d)[1], device_id_type=MESH)
        return carry

    lax.fori_loop(1, devices, greet, 0)
    RC = 128
    FC = slots // 2

    wide = select.shape[1]
    names = owners[...].astype(jnp.float32)
    ranks = jnp.zeros((1, wide), jnp.float32)
    for q in range(0, wide, RC):
        down = q + lax.broadcasted_iota(jnp.int32, (RC, wide), 0)
        over = lax.broadcasted_iota(jnp.int32, (RC, wide), 1)
        column = jnp.sum(jnp.where(down == over, names, 0.0), axis=1, keepdims=True)
        same = jnp.logical_and(column == names, down < over)
        ranks = ranks + jnp.sum(jnp.where(same, 1.0, 0.0), axis=0, keepdims=True)
    target = (names * most + ranks).astype(jnp.int32)

    def choose(q, carry):
        rows = pl.ds(pl.multiple_of(q * RC, RC), RC)
        ids = q * RC + lax.broadcasted_iota(jnp.int32, (RC, wide), 0)
        select[rows, :] = jnp.where(ids == target, 1.0, 0.0).astype(jnp.bfloat16)
        return carry

    lax.fori_loop(0, slots // RC, choose, 0)

    def first_half(e, carry):
        untangle(e)
        return carry

    lax.fori_loop(0, blocks_raw, first_half, 0)
    for b in range(NB - 2, -1, -1):
        load_inv(b).start()
    load_lower(0).start()
    load_bound(QK - 1).wait()
    for g in range(GB):
        turn(g, QK - 1)
    for q in range(QK - 1):
        load_bound(q).wait()
        turn(0, q)
        turn(1, q)
    border(0, 0)
    border(0, 1)
    pl.semaphore_wait(barrier, devices - 1)

    def remote(src, dst, ss, rs, where):
        return pltpu.make_async_remote_copy(src_ref=src, dst_ref=dst, send_sem=ss, recv_sem=rs,
                                            device_id=where, device_id_type=MESH)

    def inner_copy(s):
        return remote(sbuf.at[s], recv_a.at[s], s_sem.at[s], a_sem.at[s], {"rows": inner})

    def swap_copy(s):
        return remote(sbuf.at[s], xbuf.at[s], s_sem.at[s], x_sem.at[s], {"rows": inner})

    def back_copy(s):
        return remote(resid.at[s], resid.at[s], bs_sem.at[s], b_sem.at[s], {"rows": outer_safe})

    def pair_copy(s):
        return remote(pair_s.at[s], pair_r.at[s], ps_sem.at[s], pr_sem.at[s], {"cols": partner})

    def rs_copy(s, d):
        rows, lanes = share(0, lax.rem(m + d, M))
        return remote(rs_s.at[s, rows, lanes], rs_r.at[s, d - 1], rss_sem.at[s], rsr_sem.at[s],
                      {"cols": peer(d)})

    def all_of(s, sem):
        return pltpu.make_async_copy(rs_r.at[s], rs_r.at[s], sem.at[s])

    def ag_copy(s, k, p, d):
        rows, lanes = share(p * N + h * HALF, m)
        return remote(xt.at[k, rows, lanes], xt.at[k, rows, lanes], ags_sem.at[s], agr_sem.at[s],
                      {"cols": peer(d)})

    def fwd_copy(s, k, p):
        rows = pl.ds(pl.multiple_of(p * N + h * HALF, HALF), HALF)
        return remote(xt.at[k, rows], xt.at[k, rows], fs_sem.at[s], fr_sem.at[s], {"cols": partner})

    def half_copy(s, p):
        rows = pl.ds(pl.multiple_of(p * N + h * HALF, HALF), HALF)
        lanes = pl.ds(pl.multiple_of(partner * LB, LB), LB)
        return remote(xt.at[0, rows, lanes], xt.at[0, rows, lanes], fs_sem.at[s], fr_sem.at[s], {"cols": partner})

    def section(rows):
        return pl.ds(pl.multiple_of(rows * most, most), most)

    def send_copy(g, d):
        o, where = device(d)
        return remote(pack.at[g, section(o)], recv.at[g, section(me)], ks_sem.at[g], kr_sem.at[g], where)

    def out_copy(g):
        return pltpu.make_async_copy(recv.at[g], out.at[:, pl.ds(pl.multiple_of(g * GW, GW), GW)], o_sem.at[g])

    def split(i):
        k = NB - 1 - i // PC
        return k, lax.rem(i, PC), lax.rem(i, S)

    def piece(p):
        return pl.ds(pl.multiple_of(p * N, N), N)

    def first(i):
        k, p, s = split(i)

        @pl.when(i >= PC)
        def _():
            kb, pb, sb = split(i - PC)
            fwd_copy(sb, kb, pb).wait_recv()

        @pl.when(i == PC)
        def _():
            load_lower(0).wait()

        @pl.when(i == 2 * PC - QK)
        def _():
            for n in range(1, len(late)):
                load_lower(n).wait()

        a = lax.rem(i, PB)
        ready = pl.ds(pl.multiple_of(lax.rem(i, QK) * N, N), N)

        def hold(value):
            @pl.when(edge)
            def _():
                sbuf[s] = value.astype(jnp.bfloat16)
                inner_copy(s).start()

            @pl.when(jnp.logical_not(edge))
            def _():
                part[a] = value

        @pl.when(i < PC)
        def _():
            hold(pend[lax.rem(i // QK, 2), ready, :])

        @pl.when(i >= PC)
        def _():
            j = k + 1
            hold(pend[lax.rem(i // QK, 2), ready, :] + jnp.dot(
                xt[j, piece(p), :], tiles[unit_of(j * (j - 1) // 2 + k)], preferred_element_type=jnp.float32
            ))

    def second(i):
        k, p, s = split(i)

        @pl.when(jnp.logical_not(edge))
        def _():
            a = lax.rem(i, PB)
            inner_copy(s).wait_recv()
            both = part[a] + recv_a[s].astype(jnp.float32)
            part[a] = both
            sbuf[s] = both.astype(jnp.bfloat16)

            @pl.when(mid)
            def _():
                swap_copy(s).start()

            @pl.when(jnp.logical_not(mid))
            def _():
                inner_copy(s).start()

    def third(i):
        k, p, s = split(i)

        @pl.when(mid)
        def _():
            swap_copy(s).wait_recv()
            resid[s] = (-(part[lax.rem(i, PB)] + xbuf[s].astype(jnp.float32))).astype(jnp.bfloat16)

        @pl.when(jnp.logical_not(mid))
        def _():
            back_copy(s).wait_recv()

        @pl.when(jnp.logical_not(edge))
        def _():
            back_copy(s).start()

        @pl.when(p == 0)
        def _():
            load_inv(k).wait()

        terms = jnp.dot(resid[s], inv[k], preferred_element_type=jnp.float32)
        pair_s[s] = jnp.where(h == 0, terms[HALF:], terms[:HALF]).astype(jnp.bfloat16)
        pair_copy(s).start()
        qbuf[lax.rem(i, QB)] = jnp.where(h == 0, terms[:HALF], terms[HALF:])

    def fourth(i):
        k, p, s = split(i)
        pair_copy(s).wait_recv()
        rs_s[s] = (qbuf[lax.rem(i, QB)] + pair_r[s].astype(jnp.float32)).astype(jnp.bfloat16)
        for d in range(1, M):
            rs_copy(s, d).start()

    def fifth(i):
        k, p, s = split(i)
        lanes = share(0, m)[1]
        total = qbuf[lax.rem(i, QB), :, lanes] + pair_r[s, :, lanes].astype(jnp.float32)
        all_of(s, rsr_sem).wait()
        for d in range(1, M):
            total = total + rs_r[s, d - 1].astype(jnp.float32)
        rows, lanes = share(p * N + h * HALF, m)
        xt[k, rows, lanes] = total.astype(jnp.bfloat16)

        @pl.when(k > 0)
        def _():
            for d in range(1, M):
                ag_copy(s, k, p, d).start()

        @pl.when(k == 0)
        def _():
            half_copy(s, p).start()

    def sixth(i):
        k, p, s = split(i)

        @pl.when(k > 0)
        def _():
            all_of(s, agr_sem).wait()
            fwd_copy(s, k, p).start()

    def seventh(i):
        k, p, s = split(i)

        @pl.when(k == 0)
        def _():
            half_copy(s, p).wait_recv()

        @pl.when(jnp.logical_and(k == 0, lax.rem(p, PG) == PG - 1))
        def _():
            g = p // PG
            rows = pl.ds(pl.multiple_of(g * GW, GW), GW)
            lanes = pl.ds(pl.multiple_of(c * LB, LB), LB)
            for b in range(NB):
                own[:, b * LB:(b + 1) * LB] = xt[b, rows, lanes]

            def fill(q, carry):
                part_rows = pl.ds(pl.multiple_of(q * FC, FC), FC)
                pack[g, part_rows, :] = lax.dot_general(
                    select[part_rows, :], own[...], (((1,), (1,)), ((), ())), preferred_element_type=jnp.float32
                ).astype(jnp.bfloat16)
                return carry

            lax.fori_loop(0, slots // FC, fill, 0)

            def send(d, carry):
                send_copy(g, d).start()
                return carry

            lax.fori_loop(1, devices, send, 0)
            pltpu.make_async_copy(pack.at[g, section(me)], recv.at[g, section(me)], kr_sem.at[g]).start()

    def sends(i):
        k, p, s = split(i)
        inner_copy(s).wait_send()

        @pl.when(jnp.logical_not(edge))
        def _():
            back_copy(s).wait_send()

        pair_copy(s).wait_send()
        all_of(s, rss_sem).wait()

        @pl.when(k > 0)
        def _():
            all_of(s, ags_sem).wait()
            fwd_copy(s, k, p).wait_send()

        @pl.when(k == 0)
        def _():
            half_copy(s, p).wait_send()

    mid_lags = [min(lag, LAG_BASE) * (PC - 1) // LAG_BASE for lag in MID_LAGS]
    end_lags = [min(lag, LAG_BASE) * (PC - 1) // LAG_BASE for lag in END_LAGS]
    stages = list(zip((first, second, third, fourth, fifth, sixth), mid_lags, end_lags))
    stages.append((seventh, PC - 1, PC - 1))
    stages.append((sends, S - 1, S - 1))

    def step(t, carry):
        for stage, mid_lag, end_lag in stages:
            i = t - jnp.where(mid, mid_lag, end_lag)

            @pl.when(jnp.logical_and(i >= 0, i < items))
            def _(stage=stage, i=i):
                stage(i)

        @pl.when(t < blocks_raw)
        def _():
            untangle(blocks_raw + t)

        @pl.when(t < QK * (chunks - 1))
        def _():
            j, q = t // QK + 1, lax.rem(t, QK)

            k = NB - 1 - j // GB

            @pl.when(q < 2)
            def _():
                border(j, q)

            @pl.when(jnp.logical_and(q >= 2, q < NB - k))
            def _():
                ahead(j, k + q)

            @pl.when(jnp.logical_and(j + 1 < GB, q > 0))
            def _():
                turn(j + 1, q - 1)

        @pl.when(t == QK * (GB - 1))
        def _():
            for n in range(1, len(late)):
                load_lower(n).start()
        return carry

    lax.fori_loop(0, items + S - 1, step, 0)

    def arrive(g, carry):
        pltpu.make_async_copy(recv.at[g], recv.at[g], kr_sem.at[g]).wait()
        out_copy(g).start()
        return carry

    lax.fori_loop(0, G, arrive, 0)

    def finish(g, carry):
        sent = pack.at[g, pl.ds(0, slots - most)]
        pltpu.make_async_copy(sent, sent, ks_sem.at[g]).wait()
        out_copy(g).wait()
        return carry

    lax.fori_loop(0, G, finish, 0)


def fused(rhs, bound, border, lower, inv, owners, R, C, most):
    NB, width, sources = rhs.shape
    depth = inv.shape[2]
    devices = R * C
    N = 8 * C
    PC = sources // N
    S = PC + 4
    M = C // 2
    GW = GROUP * N
    G = sources // GW
    QK = bound.shape[0] // depth
    pairs = lower.shape[0]
    PB = max(MID_LAGS[2], END_LAGS[2]) + 2
    QB = max(MID_LAGS[4] - MID_LAGS[2], END_LAGS[4] - END_LAGS[2]) + 2
    bf, f32 = jnp.bfloat16, jnp.float32
    dma = pltpu.SemaphoreType.DMA
    anywhere = pl.BlockSpec(memory_space=pl.ANY)
    return pl.pallas_call(
        functools.partial(fused_kernel, (R, C, NB, N, PC, S, most)),
        out_shape=jax.ShapeDtypeStruct((devices * most, sources), bf),
        in_specs=[anywhere] * 5 + [pl.BlockSpec(memory_space=pltpu.VMEM)],
        out_specs=pl.BlockSpec(memory_space=pl.ANY),
        scratch_shapes=[
            pltpu.VMEM((NB * QK + 1 + max(0, pairs - 1 - QK), depth, width), bf),
            pltpu.VMEM((RAW, RAW_ROWS, 2, width), bf),
            pltpu.VMEM((sources, bound.shape[0]), bf),
            pltpu.VMEM((2, QK * N, width), f32),
            pltpu.VMEM((2, width, QK * N), f32),
            pltpu.VMEM(inv.shape, bf),
            pltpu.VMEM((NB, sources, depth), bf),
            pltpu.VMEM((PB, N, width), f32),
            pltpu.VMEM((QB, N // 2, depth), f32),
            pltpu.VMEM((S, N, width), bf),
            pltpu.VMEM((S, N, width), bf),
            pltpu.VMEM((S, N, width), bf),
            pltpu.VMEM((S, N, width), bf),
            pltpu.VMEM((S, N // 2, depth), bf),
            pltpu.VMEM((S, N // 2, depth), bf),
            pltpu.VMEM((S, N // 2, depth), bf),
            pltpu.VMEM((S, M - 1, N // 2, depth // M), bf),
            pltpu.VMEM((devices * most, owners.shape[1]), bf),
            pltpu.VMEM((GW, owners.shape[1]), bf),
            pltpu.VMEM((G, devices * most, GW), bf),
            pltpu.VMEM((G, devices * most, GW), bf),
            dma((S,)), dma((S,)), dma((S,)), dma((S,)), dma((S,)), dma((S,)), dma((S,)),
            dma((S,)), dma((S,)), dma((S,)), dma((S,)),
            dma((S,)), dma((S,)), dma((G,)), dma((RAW,)), dma((QK,)), dma((2,)), dma((NB,)), dma((pairs,)),
            dma((G,)), dma((G,)),
        ],
        compiler_params=pltpu.CompilerParams(
            collective_id=1, has_side_effects=True, vmem_limit_bytes=VMEM_BYTES
        ),
    )(rhs, bound, border, lower, inv, owners)


def local(pivot_rhs, bound_sol, border_tiles, lower_tiles, inverse_diag, owner_map):
    R = lax.axis_size("rows")
    C = lax.axis_size("cols")
    devices = R * C
    blocks, _, sources = pivot_rhs.shape
    rows_dev = owner_map.shape[1]
    per_block = rows_dev // blocks
    most = max(2, 2 * rows_dev // devices)
    pieces = 8 * C
    depth = inverse_diag.shape[2]
    if (
        R == blocks == 4 and C >= 4 and depth == sources and depth == per_block * C and bound_sol.shape[0] == 4 * depth
        and per_block % 128 == 0 and most % 32 == 0 and sources % (4 * pieces) == 0 and sources == 16 * pieces
        and bound_sol.shape[0] % RAW_ROWS == 0
    ):
        received = fused(
            pivot_rhs, bound_sol, border_tiles, lower_tiles, inverse_diag, owner_map[:, :, 0], R, C, most
        )
        return received.astype(jnp.float32)
    border = lax.dot_general(
        bound_sol, border_tiles, (((0,), (0,)), ((), ())), preferred_element_type=jnp.float32
    )
    row = lax.axis_index("rows")
    if R % blocks == 0:
        block = row // (R // blocks)
        mine = jnp.logical_and(jnp.arange(blocks) == block, lax.rem(row, R // blocks) == 0)
        rhs = lax.dynamic_index_in_dim(pivot_rhs, block, 0, keepdims=False).T[None]
        rhs = jnp.where(mine[:, None, None], rhs, 0.0)
    else:
        rhs = jnp.where(row == R // 2 - 1, pivot_rhs.transpose(0, 2, 1), 0.0)
    pend = border.transpose(1, 0, 2) - rhs
    owners = owner_map[0, :, 0]
    onehot = (owners[:, None] == jnp.arange(devices, dtype=jnp.int32)[None, :]).astype(jnp.int32)
    ranks = jnp.cumsum(onehot, axis=0) - onehot
    slots = jnp.sum(ranks * onehot, axis=1)
    target = owners * most + slots
    xt = solve(pend, lower_tiles, inverse_diag, R, C)

    own = xt
    if xt.shape[2] > per_block:
        own = lax.dynamic_slice_in_dim(xt, lax.axis_index("cols") * per_block, per_block, axis=2)
    select = (jnp.arange(devices * most, dtype=jnp.int32)[:, None] == target[None, :]).astype(jnp.bfloat16)
    select = select.reshape(devices * most, blocks, per_block)
    packed = lax.dot_general(
        select, own, (((1, 2), (0, 2)), ((), ())), preferred_element_type=jnp.float32
    ).astype(jnp.bfloat16)
    received = lax.all_to_all(
        packed.reshape(devices, most, sources), ("rows", "cols"), split_axis=0, concat_axis=0, tiled=True
    )
    return received.reshape(devices * most, sources).astype(jnp.float32)


def solution(mesh):
    placed = (
        P(None, "cols", None),
        P("rows", None),
        P("rows", None, "cols"),
        P(None, "rows", "cols"),
        P(None, "cols", "rows"),
        P(("rows", "cols"), None, None),
    )
    return jax.shard_map(
        local, mesh=mesh, in_specs=placed, out_specs=P(("rows", "cols"), None), check_vma=False
    )
```

```python
import functools

import jax
import jax.numpy as jnp
from jax import lax
from jax.experimental import pallas as pl
from jax.experimental.pallas import tpu as pltpu
from jax.sharding import PartitionSpec as P

MESH = pl.DeviceIdType.MESH
MID_LAGS = (0, 3, 6, 8, 11, 14)
END_LAGS = (0, 0, 9, 10, 12, 14)
LAG_BASE = 15
GROUP = 4
RAW = 6
PARTS = 8
RAW_ROWS = 256
VMEM_BYTES = 63 * 1024 * 1024 + 512 * 1024


def solve_kernel(dims, pend_in, lower_in, inv_in, out, pend, lower, inv, xt, part, qbuf, sbuf, recv_a, xbuf, resid,
                 pair_s, pair_r, rs_s, rs_r, s_sem, a_sem, x_sem, b_sem, bs_sem, ps_sem, pr_sem,
                 rss_sem, rsr_sem, ags_sem, agr_sem, fs_sem, fr_sem, o_sem, pl_sem, il_sem, ll_sem):
    R, C, NB, N, PC = dims
    M = C // 2
    HALF = N // 2
    depth = inv.shape[2]
    by_lanes = N // C < 16
    CH = HALF if by_lanes else HALF // M
    LW = depth // M if by_lanes else depth
    S = 2 * PC
    items = NB * PC
    z = lax.axis_index("rows")
    c = lax.axis_index("cols")
    h = lax.rem(c, 2)
    m = c // 2
    low = z < R // 2
    mid = jnp.logical_or(z == R // 2 - 1, z == R // 2)
    edge = jnp.logical_or(z == 0, z == R - 1)
    inner = jnp.where(low, z + 1, z - 1)
    outer = jnp.where(low, z - 1, z + 1)
    outer_safe = jnp.where(edge, inner, outer)
    partner = c + 1 - 2 * h

    def peer(d):
        return 2 * lax.rem(m + d, M) + h

    def share(base, q):
        if by_lanes:
            return pl.ds(pl.multiple_of(base, HALF), HALF), pl.ds(pl.multiple_of(q * LW, LW), LW)
        return pl.ds(pl.multiple_of(base + q * CH, CH), CH), slice(None)

    def load_pend(k):
        return pltpu.make_async_copy(pend_in.at[k], pend.at[k], pl_sem.at[k])

    def load_inv(k):
        return pltpu.make_async_copy(inv_in.at[k], inv.at[k], il_sem.at[k])

    load_lower = pltpu.make_async_copy(lower_in, lower, ll_sem)
    load_pend(NB - 1).start()
    load_inv(NB - 1).start()
    load_lower.start()
    for k in range(NB - 2, -1, -1):
        load_pend(k).start()
        load_inv(k).start()

    barrier = pltpu.get_barrier_semaphore()

    @pl.when(z > 0)
    def _():
        pl.semaphore_signal(barrier, inc=1, device_id={"rows": z - 1}, device_id_type=MESH)

    @pl.when(z < R - 1)
    def _():
        pl.semaphore_signal(barrier, inc=1, device_id={"rows": z + 1}, device_id_type=MESH)

    pl.semaphore_signal(barrier, inc=1, device_id={"cols": partner}, device_id_type=MESH)
    for d in range(1, M):
        pl.semaphore_signal(barrier, inc=1, device_id={"cols": peer(d)}, device_id_type=MESH)
    pl.semaphore_wait(barrier, M + jnp.where(edge, 1, 2))

    def remote(src, dst, ss, rs, where):
        return pltpu.make_async_remote_copy(src_ref=src, dst_ref=dst, send_sem=ss, recv_sem=rs,
                                            device_id=where, device_id_type=MESH)

    def inner_copy(s):
        return remote(sbuf.at[s], recv_a.at[s], s_sem.at[s], a_sem.at[s], {"rows": inner})

    def swap_copy(s):
        return remote(sbuf.at[s], xbuf.at[s], s_sem.at[s], x_sem.at[s], {"rows": inner})

    def back_copy(s):
        return remote(resid.at[s], resid.at[s], bs_sem.at[s], b_sem.at[s], {"rows": outer_safe})

    def pair_copy(s):
        return remote(pair_s.at[s], pair_r.at[s], ps_sem.at[s], pr_sem.at[s], {"cols": partner})

    def rs_copy(s, d):
        rows, lanes = share(0, lax.rem(m + d, M))
        return remote(rs_s.at[s, rows, lanes], rs_r.at[s, d - 1], rss_sem.at[s, d - 1], rsr_sem.at[s, d - 1],
                      {"cols": peer(d)})

    def ag_copy(s, k, p, d):
        rows, lanes = share(p * N + h * HALF, m)
        return remote(xt.at[k, rows, lanes], xt.at[k, rows, lanes], ags_sem.at[s, d - 1], agr_sem.at[s, d - 1],
                      {"cols": peer(d)})

    def fwd_copy(s, k, p):
        rows = pl.ds(pl.multiple_of(p * N + h * HALF, HALF), HALF)
        return remote(xt.at[k, rows], xt.at[k, rows], fs_sem.at[s], fr_sem.at[s], {"cols": partner})

    def split(i):
        k = NB - 1 - i // PC
        return k, lax.rem(i, PC), lax.rem(i, S)

    def piece(p):
        return pl.ds(pl.multiple_of(p * N, N), N)

    def first(i):
        k, p, s = split(i)

        @pl.when(i >= PC)
        def _():
            kb, pb, sb = split(i - PC)
            fwd_copy(sb, kb, pb).wait_recv()

        @pl.when(p == 0)
        def _():
            load_pend(k).wait()

        @pl.when(i == PC)
        def _():
            load_lower.wait()

        part[p] = pend[k, piece(p), :]

        def add(j, carry):
            part[p] += jnp.dot(xt[j, piece(p), :], lower[j * (j - 1) // 2 + k],
                               preferred_element_type=jnp.float32)
            return carry

        lax.fori_loop(k + 1, NB, add, 0)

        @pl.when(edge)
        def _():
            sbuf[s] = part[p].astype(jnp.bfloat16)
            inner_copy(s).start()

    def second(i):
        k, p, s = split(i)

        @pl.when(jnp.logical_not(edge))
        def _():
            inner_copy(s).wait_recv()
            part[p] += recv_a[s].astype(jnp.float32)
            sbuf[s] = part[p].astype(jnp.bfloat16)

            @pl.when(mid)
            def _():
                swap_copy(s).start()

            @pl.when(jnp.logical_not(mid))
            def _():
                inner_copy(s).start()

    def third(i):
        k, p, s = split(i)

        @pl.when(mid)
        def _():
            swap_copy(s).wait_recv()
            resid[s] = (-(part[p] + xbuf[s].astype(jnp.float32))).astype(jnp.bfloat16)

        @pl.when(jnp.logical_not(mid))
        def _():
            back_copy(s).wait_recv()

        @pl.when(jnp.logical_not(edge))
        def _():
            back_copy(s).start()

        @pl.when(p == 0)
        def _():
            load_inv(k).wait()

        qbuf[p] = jnp.dot(resid[s], inv[k], preferred_element_type=jnp.float32)
        theirs = pl.ds(pl.multiple_of((1 - h) * HALF, HALF), HALF)
        pair_s[s] = qbuf[p, theirs, :].astype(jnp.bfloat16)
        pair_copy(s).start()

    def fourth(i):
        k, p, s = split(i)
        pair_copy(s).wait_recv()
        mine = pl.ds(pl.multiple_of(h * HALF, HALF), HALF)
        both = qbuf[p, mine, :] + pair_r[s].astype(jnp.float32)
        qbuf[p, mine, :] = both
        rs_s[s] = both.astype(jnp.bfloat16)
        for d in range(1, M):
            rs_copy(s, d).start()

    def fifth(i):
        k, p, s = split(i)
        rows, lanes = share(h * HALF, m)
        total = qbuf[p, rows, lanes]
        for d in range(1, M):
            rs_copy(s, d).wait_recv()
        for d in range(1, M):
            total = total + rs_r[s, d - 1].astype(jnp.float32)
        rows, lanes = share(p * N + h * HALF, m)
        xt[k, rows, lanes] = total.astype(jnp.bfloat16)
        for d in range(1, M):
            ag_copy(s, k, p, d).start()

    def sixth(i):
        k, p, s = split(i)
        for d in range(1, M):
            ag_copy(s, k, p, d).wait_recv()
        fwd_copy(s, k, p).start()

    def sends(i):
        k, p, s = split(i)
        inner_copy(s).wait_send()

        @pl.when(jnp.logical_not(edge))
        def _():
            back_copy(s).wait_send()

        pair_copy(s).wait_send()
        for d in range(1, M):
            rs_copy(s, d).wait_send()
        for d in range(1, M):
            ag_copy(s, k, p, d).wait_send()
        fwd_copy(s, k, p).wait_send()

    mid_lags = [min(lag, LAG_BASE) * (PC - 1) // LAG_BASE for lag in MID_LAGS]
    end_lags = [min(lag, LAG_BASE) * (PC - 1) // LAG_BASE for lag in END_LAGS]
    stages = list(zip((first, second, third, fourth, fifth, sixth), mid_lags, end_lags))
    stages.append((sends, PC + PC // 2, PC + PC // 2))

    def step(t, carry):
        for stage, mid_lag, end_lag in stages:
            i = t - jnp.where(mid, mid_lag, end_lag)

            @pl.when(jnp.logical_and(i >= 0, i < items))
            def _(stage=stage, i=i):
                stage(i)
        return carry

    lax.fori_loop(0, items + PC + PC // 2, step, 0)

    def last(i, carry):
        k, p, s = split(i)
        fwd_copy(s, k, p).wait_recv()
        return carry

    lax.fori_loop(items - PC, items, last, 0)
    cut = out.shape[2]
    source = xt
    if cut < depth:
        source = xt.at[:, :, pl.ds(pl.multiple_of(c * cut, cut), cut)]
    write = pltpu.make_async_copy(source, out, o_sem)
    write.start()
    write.wait()


def solve(pend, lower, inv, R, C):
    NB, sources, width = pend.shape
    depth = inv.shape[2]
    wide = depth % (64 * C) == 0
    N = min(8 * C if wide else 16 * C, sources // 2)
    PC = sources // N
    S = 2 * PC
    M = C // 2
    bf, f32 = jnp.bfloat16, jnp.float32
    dma = pltpu.SemaphoreType.DMA
    anywhere = pl.BlockSpec(memory_space=pl.ANY)
    cut = depth // C if depth % (128 * C) == 0 else depth
    return pl.pallas_call(
        functools.partial(solve_kernel, (R, C, NB, N, PC)),
        out_shape=jax.ShapeDtypeStruct((NB, sources, cut), bf),
        in_specs=[anywhere, anywhere, anywhere],
        out_specs=pl.BlockSpec(memory_space=pl.ANY),
        scratch_shapes=[
            pltpu.VMEM(pend.shape, f32),
            pltpu.VMEM(lower.shape, bf),
            pltpu.VMEM(inv.shape, bf),
            pltpu.VMEM((NB, sources, depth), bf),
            pltpu.VMEM((PC, N, width), f32),
            pltpu.VMEM((PC, N, depth), f32),
            pltpu.VMEM((S, N, width), bf),
            pltpu.VMEM((S, N, width), bf),
            pltpu.VMEM((S, N, width), bf),
            pltpu.VMEM((S, N, width), bf),
            pltpu.VMEM((S, N // 2, depth), bf),
            pltpu.VMEM((S, N // 2, depth), bf),
            pltpu.VMEM((S, N // 2, depth), bf),
            pltpu.VMEM((S, M - 1) + ((N // 2, depth // M) if N // C < 16 else (N // C, depth)), bf),
            dma((S,)), dma((S,)), dma((S,)), dma((S,)), dma((S,)), dma((S,)), dma((S,)),
            dma((S, M - 1)), dma((S, M - 1)), dma((S, M - 1)), dma((S, M - 1)),
            dma((S,)), dma((S,)), dma, dma((NB,)), dma((NB,)), dma,
        ],
        compiler_params=pltpu.CompilerParams(
            collective_id=0, has_side_effects=True, vmem_limit_bytes=60 * 1024 * 1024
        ),
    )(pend, lower, inv)


def fused_kernel(dims, rhs_in, bound_in, border_in, lower_in, inv_in, owners, out, tiles, raw, bound, pend, rhs, inv, xt,
                 part, qbuf, sbuf, recv_a, xbuf, resid, pair_s, pair_r, rs_s, rs_r, select, own, pack, recv,
                 s_sem, a_sem, x_sem, b_sem, bs_sem, ps_sem, pr_sem, rss_sem, rsr_sem, ags_sem, agr_sem, fs_sem, fr_sem,
                 o_sem, raw_sem, bd_sem, rhs_sem, il_sem, ll_sem, ks_sem, kr_sem):
    R, C, NB, N, PC, S, most = dims
    devices = R * C
    M = C // 2
    HALF = N // 2
    depth = inv.shape[2]
    LW = depth // M
    LB = depth // C
    G, slots, GW = pack.shape
    PG = GW // N
    PB = part.shape[0]
    QB = qbuf.shape[0]
    NR, RB = raw.shape[:2]
    QK = bound.shape[1] // depth
    BW = pend.shape[1]
    GB = PC // QK
    chunks = NB * GB
    blocks_raw = bound.shape[1] // RB
    late = []
    for earlier in range(NB - 2, -1, -1):
        late += [(later, earlier) for later in range(earlier + 1, NB)]
    late_unit = {}
    for n, (later, earlier) in enumerate(late):
        unit = NB * QK if n == 0 else (NB - 1) * QK + n - 1
        if n > QK:
            unit = NB * QK + n - QK
        late_unit[later * (later - 1) // 2 + earlier] = unit
    items = NB * PC
    z = lax.axis_index("rows")
    c = lax.axis_index("cols")
    h = lax.rem(c, 2)
    m = c // 2
    low = z < R // 2
    mid = jnp.logical_or(z == R // 2 - 1, z == R // 2)
    edge = jnp.logical_or(z == 0, z == R - 1)
    inner = jnp.where(low, z + 1, z - 1)
    outer = jnp.where(low, z - 1, z + 1)
    outer_safe = jnp.where(edge, inner, outer)
    partner = c + 1 - 2 * h
    me = z * C + c

    def peer(d):
        return 2 * lax.rem(m + d, M) + h

    def share(base, q):
        return pl.ds(pl.multiple_of(base, HALF), HALF), pl.ds(pl.multiple_of(q * LW, LW), LW)

    def load_inv(k):
        return pltpu.make_async_copy(inv_in.at[k], inv.at[k], il_sem.at[k])

    def load_lower(n):
        pair = late[n][0] * (late[n][0] - 1) // 2 + late[n][1]
        return pltpu.make_async_copy(lower_in.at[pair], tiles.at[late_unit[pair]], ll_sem.at[n])

    def load_raw(e):
        pair = NB // 2 - 1 - e // blocks_raw
        rows = pl.ds(pl.multiple_of(lax.rem(e, blocks_raw) * RB, RB), RB)
        slot = lax.rem(e, NR)
        return pltpu.make_async_copy(border_in.at[rows, pl.ds(2 * pair, 2), :], raw.at[slot], raw_sem.at[slot])

    def load_bound(q):
        return pltpu.make_async_copy(bound_in.at[pl.ds(q * depth, depth)], xt.at[q], bd_sem.at[q])

    def load_rhs(g):
        lanes = pl.ds(pl.multiple_of(g * BW, BW), BW)
        slot = lax.rem(g, 2)
        return pltpu.make_async_copy(rhs_in.at[z, :, lanes], rhs.at[slot], rhs_sem.at[slot])

    def untangle(e):
        pair = NB // 2 - 1 - e // blocks_raw
        start = lax.rem(e, blocks_raw) * RB
        rows = pl.ds(pl.multiple_of(lax.rem(start, depth), RB), RB)
        load_raw(e).wait()
        both = jnp.swapaxes(raw[lax.rem(e, NR)], 0, 1)
        for b in range(2):
            tiles[(2 * pair + b) * QK + start // depth, rows, :] = both[b]

        @pl.when(e + NR < NB // 2 * blocks_raw)
        def _():
            load_raw(e + NR).start()

    def turn(g, q):
        rows = pl.ds(pl.multiple_of(g * BW, BW), BW)
        lanes = pl.ds(pl.multiple_of(q * depth, depth), depth)
        bound[rows, lanes] = xt[q, :, rows].T

    def border(j, half):
        k = NB - 1 - j // GB
        g = lax.rem(j, GB)
        slot = lax.rem(j, 2)
        rows = pl.ds(pl.multiple_of(g * BW, BW), BW)
        width = pend.shape[2]
        lanes = pl.ds(pl.multiple_of(half * (width // 2), width // 2), width // 2)
        block = tiles[pl.ds(k * QK, QK), :, lanes].reshape(QK * depth, width // 2)
        pend[slot, :, lanes] = jnp.dot(bound[rows, :], block, preferred_element_type=jnp.float32)

        @pl.when(jnp.logical_and(half == 1, k == z))
        def _():
            load_rhs(g).wait()
            pend[slot] -= rhs[lax.rem(g, 2)].T

            @pl.when(g + 2 < GB)
            def _():
                load_rhs(g + 2).start()

    def unit_of(pair):
        unit = late_unit[0]
        for n in range(1, len(late)):
            unit = jnp.where(pair == n, late_unit[n], unit)
        return unit

    def ahead(j, half, later):
        k = NB - 1 - j // GB
        rows = pl.ds(pl.multiple_of(lax.rem(j, GB) * BW, BW), BW)
        width = pend.shape[2]
        lanes = pl.ds(pl.multiple_of(half * (width // 2), width // 2), width // 2)
        pend[lax.rem(j, 2), :, lanes] += jnp.dot(
            xt[later, rows, :], tiles[unit_of(later * (later - 1) // 2 + k), :, lanes],
            preferred_element_type=jnp.float32,
        )

    def first_raw(e, carry):
        load_raw(e).start()
        return carry

    lax.fori_loop(0, NR, first_raw, 0)
    order = [QK - 1] + list(range(QK - 1))
    load_bound(order[0]).start()
    load_bound(order[1]).start()
    load_rhs(0).start()
    load_rhs(1).start()
    load_inv(NB - 1).start()

    barrier = pltpu.get_barrier_semaphore()

    def device(d):
        o = lax.rem(me + d, devices)
        return o, {"rows": o // C, "cols": lax.rem(o, C)}

    def greet(d, carry):
        pl.semaphore_signal(barrier, inc=1, device_id=device(d)[1], device_id_type=MESH)
        return carry

    lax.fori_loop(1, devices, greet, 0)
    RC = 128
    FC = slots // 2

    wide = select.shape[1]
    names = owners[...].astype(jnp.float32)
    ranks = jnp.zeros((1, wide), jnp.float32)
    for q in range(0, wide, RC):
        down = q + lax.broadcasted_iota(jnp.int32, (RC, wide), 0)
        over = lax.broadcasted_iota(jnp.int32, (RC, wide), 1)
        column = jnp.sum(jnp.where(down == over, names, 0.0), axis=1, keepdims=True)
        same = jnp.logical_and(column == names, down < over)
        ranks = ranks + jnp.sum(jnp.where(same, 1.0, 0.0), axis=0, keepdims=True)
    target = (names * most + ranks).astype(jnp.int32)

    def choose(q, carry):
        rows = pl.ds(pl.multiple_of(q * RC, RC), RC)
        ids = q * RC + lax.broadcasted_iota(jnp.int32, (RC, wide), 0)
        select[rows, :] = jnp.where(ids == target, 1.0, 0.0).astype(jnp.bfloat16)
        return carry

    lax.fori_loop(0, slots // RC, choose, 0)

    def first_half(e, carry):
        untangle(e)
        return carry

    stretch = blocks_raw // QK
    for n in range(QK):
        lax.fori_loop(n * stretch, (n + 1) * stretch, first_half, 0)
        if n + 2 < QK:
            load_bound(order[n + 2]).start()
        load_bound(order[n]).wait()
        for g in range(GB if n == 0 else 2):
            turn(g, order[n])
    for b in range(NB - 2, -1, -1):
        load_inv(b).start()
    load_lower(0).start()
    border(0, 0)
    border(0, 1)
    pl.semaphore_wait(barrier, devices - 1)

    def remote(src, dst, ss, rs, where):
        return pltpu.make_async_remote_copy(src_ref=src, dst_ref=dst, send_sem=ss, recv_sem=rs,
                                            device_id=where, device_id_type=MESH)

    def inner_copy(s):
        return remote(sbuf.at[s], recv_a.at[s], s_sem.at[s], a_sem.at[s], {"rows": inner})

    def swap_copy(s):
        return remote(sbuf.at[s], xbuf.at[s], s_sem.at[s], x_sem.at[s], {"rows": inner})

    def back_copy(s):
        return remote(resid.at[s], resid.at[s], bs_sem.at[s], b_sem.at[s], {"rows": outer_safe})

    def pair_copy(s):
        return remote(pair_s.at[s], pair_r.at[s], ps_sem.at[s], pr_sem.at[s], {"cols": partner})

    def rs_copy(s, d):
        rows, lanes = share(0, lax.rem(m + d, M))
        return remote(rs_s.at[s, rows, lanes], rs_r.at[s, d - 1], rss_sem.at[s], rsr_sem.at[s],
                      {"cols": peer(d)})

    def all_of(s, sem):
        return pltpu.make_async_copy(rs_r.at[s], rs_r.at[s], sem.at[s])

    def ag_copy(s, k, p, d):
        rows, lanes = share(p * N + h * HALF, m)
        return remote(xt.at[k, rows, lanes], xt.at[k, rows, lanes], ags_sem.at[s], agr_sem.at[s],
                      {"cols": peer(d)})

    def fwd_copy(s, k, p):
        rows = pl.ds(pl.multiple_of(p * N + h * HALF, HALF), HALF)
        return remote(xt.at[k, rows], xt.at[k, rows], fs_sem.at[s], fr_sem.at[s], {"cols": partner})

    def half_copy(s, p):
        rows = pl.ds(pl.multiple_of(p * N + h * HALF, HALF), HALF)
        lanes = pl.ds(pl.multiple_of(partner * LB, LB), LB)
        return remote(xt.at[0, rows, lanes], xt.at[0, rows, lanes], fs_sem.at[s], fr_sem.at[s], {"cols": partner})

    def section(rows):
        return pl.ds(pl.multiple_of(rows * most, most), most)

    def send_copy(g, d):
        o, where = device(d)
        return remote(pack.at[g, section(o)], recv.at[g, section(me)], ks_sem.at[g], kr_sem.at[g], where)

    def out_copy(g):
        return pltpu.make_async_copy(recv.at[g], out.at[:, pl.ds(pl.multiple_of(g * GW, GW), GW)], o_sem.at[g])

    def split(i):
        k = NB - 1 - i // PC
        return k, lax.rem(i, PC), lax.rem(i, S)

    def piece(p):
        return pl.ds(pl.multiple_of(p * N, N), N)

    def first(i):
        k, p, s = split(i)

        @pl.when(i >= PC)
        def _():
            kb, pb, sb = split(i - PC)
            fwd_copy(sb, kb, pb).wait_recv()

        @pl.when(i == PC)
        def _():
            load_lower(0).wait()

        @pl.when(i == 2 * PC - QK)
        def _():
            for n in range(1, len(late)):
                load_lower(n).wait()

        a = lax.rem(i, PB)
        ready = pl.ds(pl.multiple_of(lax.rem(i, QK) * N, N), N)

        def hold(value):
            @pl.when(edge)
            def _():
                sbuf[s] = value.astype(jnp.bfloat16)
                inner_copy(s).start()

            @pl.when(jnp.logical_not(edge))
            def _():
                part[a] = value

        @pl.when(i < PC)
        def _():
            hold(pend[lax.rem(i // QK, 2), ready, :])

        @pl.when(i >= PC)
        def _():
            j = k + 1
            hold(pend[lax.rem(i // QK, 2), ready, :] + jnp.dot(
                xt[j, piece(p), :], tiles[unit_of(j * (j - 1) // 2 + k)], preferred_element_type=jnp.float32
            ))

    def second(i):
        k, p, s = split(i)

        @pl.when(jnp.logical_not(edge))
        def _():
            a = lax.rem(i, PB)
            inner_copy(s).wait_recv()
            both = part[a] + recv_a[s].astype(jnp.float32)
            part[a] = both
            sbuf[s] = both.astype(jnp.bfloat16)

            @pl.when(mid)
            def _():
                swap_copy(s).start()

            @pl.when(jnp.logical_not(mid))
            def _():
                inner_copy(s).start()

    def third(i):
        k, p, s = split(i)

        @pl.when(mid)
        def _():
            swap_copy(s).wait_recv()
            resid[s] = (-(part[lax.rem(i, PB)] + xbuf[s].astype(jnp.float32))).astype(jnp.bfloat16)

        @pl.when(jnp.logical_not(mid))
        def _():
            back_copy(s).wait_recv()

        @pl.when(jnp.logical_not(edge))
        def _():
            back_copy(s).start()

        @pl.when(p == 0)
        def _():
            load_inv(k).wait()

        terms = jnp.dot(resid[s], inv[k], preferred_element_type=jnp.float32)
        pair_s[s] = jnp.where(h == 0, terms[HALF:], terms[:HALF]).astype(jnp.bfloat16)
        pair_copy(s).start()
        qbuf[lax.rem(i, QB)] = jnp.where(h == 0, terms[:HALF], terms[HALF:])

    def fourth(i):
        k, p, s = split(i)
        pair_copy(s).wait_recv()
        rs_s[s] = (qbuf[lax.rem(i, QB)] + pair_r[s].astype(jnp.float32)).astype(jnp.bfloat16)
        for d in range(1, M):
            rs_copy(s, d).start()

    def fifth(i):
        k, p, s = split(i)
        lanes = share(0, m)[1]
        total = qbuf[lax.rem(i, QB), :, lanes] + pair_r[s, :, lanes].astype(jnp.float32)
        all_of(s, rsr_sem).wait()
        for d in range(1, M):
            total = total + rs_r[s, d - 1].astype(jnp.float32)
        rows, lanes = share(p * N + h * HALF, m)
        xt[k, rows, lanes] = total.astype(jnp.bfloat16)

        @pl.when(k > 0)
        def _():
            for d in range(1, M):
                ag_copy(s, k, p, d).start()

        @pl.when(k == 0)
        def _():
            half_copy(s, p).start()

    def sixth(i):
        k, p, s = split(i)

        @pl.when(k > 0)
        def _():
            all_of(s, agr_sem).wait()
            fwd_copy(s, k, p).start()

    def seventh(i):
        k, p, s = split(i)

        @pl.when(k == 0)
        def _():
            half_copy(s, p).wait_recv()

        @pl.when(jnp.logical_and(k == 0, lax.rem(p, PG) == PG - 1))
        def _():
            g = p // PG
            rows = pl.ds(pl.multiple_of(g * GW, GW), GW)
            lanes = pl.ds(pl.multiple_of(c * LB, LB), LB)
            for b in range(NB):
                own[:, b * LB:(b + 1) * LB] = xt[b, rows, lanes]

            def fill(q, carry):
                part_rows = pl.ds(pl.multiple_of(q * FC, FC), FC)
                pack[g, part_rows, :] = lax.dot_general(
                    select[part_rows, :], own[...], (((1,), (1,)), ((), ())), preferred_element_type=jnp.float32
                ).astype(jnp.bfloat16)
                return carry

            lax.fori_loop(0, slots // FC, fill, 0)

            def send(d, carry):
                send_copy(g, d).start()
                return carry

            lax.fori_loop(1, devices, send, 0)
            pltpu.make_async_copy(pack.at[g, section(me)], recv.at[g, section(me)], kr_sem.at[g]).start()

    def sends(i):
        k, p, s = split(i)
        inner_copy(s).wait_send()

        @pl.when(jnp.logical_not(edge))
        def _():
            back_copy(s).wait_send()

        pair_copy(s).wait_send()
        all_of(s, rss_sem).wait()

        @pl.when(k > 0)
        def _():
            all_of(s, ags_sem).wait()
            fwd_copy(s, k, p).wait_send()

        @pl.when(k == 0)
        def _():
            half_copy(s, p).wait_send()

    mid_lags = [min(lag, LAG_BASE) * (PC - 1) // LAG_BASE for lag in MID_LAGS]
    end_lags = [min(lag, LAG_BASE) * (PC - 1) // LAG_BASE for lag in END_LAGS]
    stages = list(zip((first, second, third, fourth, fifth, sixth), mid_lags, end_lags))
    stages.append((seventh, PC - 1, PC - 1))
    stages.append((sends, S - 1, S - 1))

    def fill_in(t):
        @pl.when(t < blocks_raw)
        def _():
            untangle(blocks_raw + t)

        @pl.when(t < QK * (chunks - 1))
        def _():
            j, q = t // QK + 1, lax.rem(t, QK)

            k = NB - 1 - j // GB

            @pl.when(lax.rem(q, 2) == 0)
            def _():
                border(j, q // 2)

            @pl.when(jnp.logical_and(lax.rem(q, 2) == 1, k + 2 < NB))
            def _():
                ahead(j, q // 2, k + 2)

            @pl.when(jnp.logical_and(lax.rem(q, 2) == 1, k + 3 < NB))
            def _():
                ahead(j, q // 2, k + 3)

            @pl.when(jnp.logical_and(j + 1 < GB, q > 0))
            def _():
                turn(j + 1, q - 1)


    def step(t, carry):
        for n, (stage, mid_lag, end_lag) in enumerate(stages):
            if n == 1:
                fill_in(t)
            i = t - jnp.where(mid, mid_lag, end_lag)

            @pl.when(jnp.logical_and(i >= 0, i < items))
            def _(stage=stage, i=i):
                stage(i)

        @pl.when(t == QK * (GB - 1))
        def _():
            for n in range(1, len(late)):
                load_lower(n).start()
        return carry

    lax.fori_loop(0, items + S - 1, step, 0)

    def arrive(g, carry):
        pltpu.make_async_copy(recv.at[g], recv.at[g], kr_sem.at[g]).wait()
        out_copy(g).start()
        return carry

    lax.fori_loop(0, G, arrive, 0)

    def finish(g, carry):
        sent = pack.at[g, pl.ds(0, slots - most)]
        pltpu.make_async_copy(sent, sent, ks_sem.at[g]).wait()
        out_copy(g).wait()
        return carry

    lax.fori_loop(0, G, finish, 0)


def fused(rhs, bound, border, lower, inv, owners, R, C, most):
    NB, width, sources = rhs.shape
    depth = inv.shape[2]
    devices = R * C
    N = 8 * C
    PC = sources // N
    S = PC + 4
    M = C // 2
    GW = GROUP * N
    G = sources // GW
    QK = bound.shape[0] // depth
    pairs = lower.shape[0]
    PB = max(MID_LAGS[2], END_LAGS[2]) + 2
    QB = max(MID_LAGS[4] - MID_LAGS[2], END_LAGS[4] - END_LAGS[2]) + 2
    bf, f32 = jnp.bfloat16, jnp.float32
    dma = pltpu.SemaphoreType.DMA
    anywhere = pl.BlockSpec(memory_space=pl.ANY)
    return pl.pallas_call(
        functools.partial(fused_kernel, (R, C, NB, N, PC, S, most)),
        out_shape=jax.ShapeDtypeStruct((devices * most, sources), bf),
        in_specs=[anywhere] * 5 + [pl.BlockSpec(memory_space=pltpu.VMEM)],
        out_specs=pl.BlockSpec(memory_space=pl.ANY),
        scratch_shapes=[
            pltpu.VMEM((NB * QK + 1 + max(0, pairs - 1 - QK), depth, width), bf),
            pltpu.VMEM((RAW, RAW_ROWS, 2, width), bf),
            pltpu.VMEM((sources, bound.shape[0]), bf),
            pltpu.VMEM((2, QK * N, width), f32),
            pltpu.VMEM((2, width, QK * N), f32),
            pltpu.VMEM(inv.shape, bf),
            pltpu.VMEM((NB, sources, depth), bf),
            pltpu.VMEM((PB, N, width), f32),
            pltpu.VMEM((QB, N // 2, depth), f32),
            pltpu.VMEM((S, N, width), bf),
            pltpu.VMEM((S, N, width), bf),
            pltpu.VMEM((S, N, width), bf),
            pltpu.VMEM((S, N, width), bf),
            pltpu.VMEM((S, N // 2, depth), bf),
            pltpu.VMEM((S, N // 2, depth), bf),
            pltpu.VMEM((S, N // 2, depth), bf),
            pltpu.VMEM((S, M - 1, N // 2, depth // M), bf),
            pltpu.VMEM((devices * most, owners.shape[1]), bf),
            pltpu.VMEM((GW, owners.shape[1]), bf),
            pltpu.VMEM((G, devices * most, GW), bf),
            pltpu.VMEM((G, devices * most, GW), bf),
            dma((S,)), dma((S,)), dma((S,)), dma((S,)), dma((S,)), dma((S,)), dma((S,)),
            dma((S,)), dma((S,)), dma((S,)), dma((S,)),
            dma((S,)), dma((S,)), dma((G,)), dma((RAW,)), dma((QK,)), dma((2,)), dma((NB,)), dma((pairs,)),
            dma((G,)), dma((G,)),
        ],
        compiler_params=pltpu.CompilerParams(
            collective_id=1, has_side_effects=True, vmem_limit_bytes=VMEM_BYTES
        ),
    )(rhs, bound, border, lower, inv, owners)


def widen_kernel(source, out, narrow, full, in_sem, out_sem):
    parts = in_sem.shape[0]
    rows = source.shape[0] // parts

    def take(n):
        part = pl.ds(n * rows, rows)
        return pltpu.make_async_copy(source.at[part], narrow.at[part], in_sem.at[n])

    def give(n):
        part = pl.ds(n * rows, rows)
        return pltpu.make_async_copy(full.at[part], out.at[part], out_sem.at[n])

    for n in range(parts):
        take(n).start()
    for n in range(parts):
        take(n).wait()
        full[n * rows:(n + 1) * rows, :] = narrow[n * rows:(n + 1) * rows, :].astype(jnp.float32)
        give(n).start()
    for n in range(parts):
        give(n).wait()


def widen(values):
    dma = pltpu.SemaphoreType.DMA
    return pl.pallas_call(
        widen_kernel,
        out_shape=jax.ShapeDtypeStruct(values.shape, jnp.float32),
        in_specs=[pl.BlockSpec(memory_space=pl.ANY)],
        out_specs=pl.BlockSpec(memory_space=pl.ANY),
        scratch_shapes=[
            pltpu.VMEM(values.shape, values.dtype), pltpu.VMEM(values.shape, jnp.float32), dma((PARTS,)), dma((PARTS,)),
        ],
    )(values)


def local(pivot_rhs, bound_sol, border_tiles, lower_tiles, inverse_diag, owner_map):
    R = lax.axis_size("rows")
    C = lax.axis_size("cols")
    devices = R * C
    blocks, _, sources = pivot_rhs.shape
    rows_dev = owner_map.shape[1]
    per_block = rows_dev // blocks
    most = max(2, 2 * rows_dev // devices)
    pieces = 8 * C
    depth = inverse_diag.shape[2]
    if (
        R == blocks == 4 and C >= 4 and depth == sources and depth == per_block * C and bound_sol.shape[0] == 4 * depth
        and per_block % 128 == 0 and most % 32 == 0 and sources % (4 * pieces) == 0 and sources == 16 * pieces
        and bound_sol.shape[0] % RAW_ROWS == 0
    ):
        received = fused(
            pivot_rhs, bound_sol, border_tiles, lower_tiles, inverse_diag, owner_map[:, :, 0], R, C, most
        )
        return widen(received)
    border = lax.dot_general(
        bound_sol, border_tiles, (((0,), (0,)), ((), ())), preferred_element_type=jnp.float32
    )
    row = lax.axis_index("rows")
    if R % blocks == 0:
        block = row // (R // blocks)
        mine = jnp.logical_and(jnp.arange(blocks) == block, lax.rem(row, R // blocks) == 0)
        rhs = lax.dynamic_index_in_dim(pivot_rhs, block, 0, keepdims=False).T[None]
        rhs = jnp.where(mine[:, None, None], rhs, 0.0)
    else:
        rhs = jnp.where(row == R // 2 - 1, pivot_rhs.transpose(0, 2, 1), 0.0)
    pend = border.transpose(1, 0, 2) - rhs
    owners = owner_map[0, :, 0]
    onehot = (owners[:, None] == jnp.arange(devices, dtype=jnp.int32)[None, :]).astype(jnp.int32)
    ranks = jnp.cumsum(onehot, axis=0) - onehot
    slots = jnp.sum(ranks * onehot, axis=1)
    target = owners * most + slots
    xt = solve(pend, lower_tiles, inverse_diag, R, C)

    own = xt
    if xt.shape[2] > per_block:
        own = lax.dynamic_slice_in_dim(xt, lax.axis_index("cols") * per_block, per_block, axis=2)
    select = (jnp.arange(devices * most, dtype=jnp.int32)[:, None] == target[None, :]).astype(jnp.bfloat16)
    select = select.reshape(devices * most, blocks, per_block)
    packed = lax.dot_general(
        select, own, (((1, 2), (0, 2)), ((), ())), preferred_element_type=jnp.float32
    ).astype(jnp.bfloat16)
    received = lax.all_to_all(
        packed.reshape(devices, most, sources), ("rows", "cols"), split_axis=0, concat_axis=0, tiled=True
    )
    return received.reshape(devices * most, sources).astype(jnp.float32)


def solution(mesh):
    placed = (
        P(None, "cols", None),
        P("rows", None),
        P("rows", None, "cols"),
        P(None, "rows", "cols"),
        P(None, "cols", "rows"),
        P(("rows", "cols"), None, None),
    )
    return jax.shard_map(
        local, mesh=mesh, in_specs=placed, out_specs=P(("rows", "cols"), None), check_vma=False
    )
```

```python
import functools

import jax
import jax.numpy as jnp
from jax import lax
from jax.experimental import pallas as pl
from jax.experimental.pallas import tpu as pltpu
from jax.sharding import PartitionSpec as P

MESH = pl.DeviceIdType.MESH
MID_LAGS = (0, 3, 6, 8, 11, 14)
END_LAGS = (0, 0, 9, 10, 12, 14)
LAG_BASE = 15
GROUP = 4
RAW = 6
PARTS = 8
RAW_ROWS = 256
VMEM_BYTES = 63 * 1024 * 1024 + 512 * 1024


def solve_kernel(dims, pend_in, lower_in, inv_in, out, pend, lower, inv, xt, part, qbuf, sbuf, recv_a, xbuf, resid,
                 pair_s, pair_r, rs_s, rs_r, s_sem, a_sem, x_sem, b_sem, bs_sem, ps_sem, pr_sem,
                 rss_sem, rsr_sem, ags_sem, agr_sem, fs_sem, fr_sem, o_sem, pl_sem, il_sem, ll_sem):
    R, C, NB, N, PC = dims
    M = C // 2
    HALF = N // 2
    depth = inv.shape[2]
    by_lanes = N // C < 16
    CH = HALF if by_lanes else HALF // M
    LW = depth // M if by_lanes else depth
    S = 2 * PC
    items = NB * PC
    z = lax.axis_index("rows")
    c = lax.axis_index("cols")
    h = lax.rem(c, 2)
    m = c // 2
    low = z < R // 2
    mid = jnp.logical_or(z == R // 2 - 1, z == R // 2)
    edge = jnp.logical_or(z == 0, z == R - 1)
    inner = jnp.where(low, z + 1, z - 1)
    outer = jnp.where(low, z - 1, z + 1)
    outer_safe = jnp.where(edge, inner, outer)
    partner = c + 1 - 2 * h

    def peer(d):
        return 2 * lax.rem(m + d, M) + h

    def share(base, q):
        if by_lanes:
            return pl.ds(pl.multiple_of(base, HALF), HALF), pl.ds(pl.multiple_of(q * LW, LW), LW)
        return pl.ds(pl.multiple_of(base + q * CH, CH), CH), slice(None)

    def load_pend(k):
        return pltpu.make_async_copy(pend_in.at[k], pend.at[k], pl_sem.at[k])

    def load_inv(k):
        return pltpu.make_async_copy(inv_in.at[k], inv.at[k], il_sem.at[k])

    load_lower = pltpu.make_async_copy(lower_in, lower, ll_sem)
    load_pend(NB - 1).start()
    load_inv(NB - 1).start()
    load_lower.start()
    for k in range(NB - 2, -1, -1):
        load_pend(k).start()
        load_inv(k).start()

    barrier = pltpu.get_barrier_semaphore()

    @pl.when(z > 0)
    def _():
        pl.semaphore_signal(barrier, inc=1, device_id={"rows": z - 1}, device_id_type=MESH)

    @pl.when(z < R - 1)
    def _():
        pl.semaphore_signal(barrier, inc=1, device_id={"rows": z + 1}, device_id_type=MESH)

    pl.semaphore_signal(barrier, inc=1, device_id={"cols": partner}, device_id_type=MESH)
    for d in range(1, M):
        pl.semaphore_signal(barrier, inc=1, device_id={"cols": peer(d)}, device_id_type=MESH)
    pl.semaphore_wait(barrier, M + jnp.where(edge, 1, 2))

    def remote(src, dst, ss, rs, where):
        return pltpu.make_async_remote_copy(src_ref=src, dst_ref=dst, send_sem=ss, recv_sem=rs,
                                            device_id=where, device_id_type=MESH)

    def inner_copy(s):
        return remote(sbuf.at[s], recv_a.at[s], s_sem.at[s], a_sem.at[s], {"rows": inner})

    def swap_copy(s):
        return remote(sbuf.at[s], xbuf.at[s], s_sem.at[s], x_sem.at[s], {"rows": inner})

    def back_copy(s):
        return remote(resid.at[s], resid.at[s], bs_sem.at[s], b_sem.at[s], {"rows": outer_safe})

    def pair_copy(s):
        return remote(pair_s.at[s], pair_r.at[s], ps_sem.at[s], pr_sem.at[s], {"cols": partner})

    def rs_copy(s, d):
        rows, lanes = share(0, lax.rem(m + d, M))
        return remote(rs_s.at[s, rows, lanes], rs_r.at[s, d - 1], rss_sem.at[s, d - 1], rsr_sem.at[s, d - 1],
                      {"cols": peer(d)})

    def ag_copy(s, k, p, d):
        rows, lanes = share(p * N + h * HALF, m)
        return remote(xt.at[k, rows, lanes], xt.at[k, rows, lanes], ags_sem.at[s, d - 1], agr_sem.at[s, d - 1],
                      {"cols": peer(d)})

    def fwd_copy(s, k, p):
        rows = pl.ds(pl.multiple_of(p * N + h * HALF, HALF), HALF)
        return remote(xt.at[k, rows], xt.at[k, rows], fs_sem.at[s], fr_sem.at[s], {"cols": partner})

    def split(i):
        k = NB - 1 - i // PC
        return k, lax.rem(i, PC), lax.rem(i, S)

    def piece(p):
        return pl.ds(pl.multiple_of(p * N, N), N)

    def first(i):
        k, p, s = split(i)

        @pl.when(i >= PC)
        def _():
            kb, pb, sb = split(i - PC)
            fwd_copy(sb, kb, pb).wait_recv()

        @pl.when(p == 0)
        def _():
            load_pend(k).wait()

        @pl.when(i == PC)
        def _():
            load_lower.wait()

        part[p] = pend[k, piece(p), :]

        def add(j, carry):
            part[p] += jnp.dot(xt[j, piece(p), :], lower[j * (j - 1) // 2 + k],
                               preferred_element_type=jnp.float32)
            return carry

        lax.fori_loop(k + 1, NB, add, 0)

        @pl.when(edge)
        def _():
            sbuf[s] = part[p].astype(jnp.bfloat16)
            inner_copy(s).start()

    def second(i):
        k, p, s = split(i)

        @pl.when(jnp.logical_not(edge))
        def _():
            inner_copy(s).wait_recv()
            part[p] += recv_a[s].astype(jnp.float32)
            sbuf[s] = part[p].astype(jnp.bfloat16)

            @pl.when(mid)
            def _():
                swap_copy(s).start()

            @pl.when(jnp.logical_not(mid))
            def _():
                inner_copy(s).start()

    def third(i):
        k, p, s = split(i)

        @pl.when(mid)
        def _():
            swap_copy(s).wait_recv()
            resid[s] = (-(part[p] + xbuf[s].astype(jnp.float32))).astype(jnp.bfloat16)

        @pl.when(jnp.logical_not(mid))
        def _():
            back_copy(s).wait_recv()

        @pl.when(jnp.logical_not(edge))
        def _():
            back_copy(s).start()

        @pl.when(p == 0)
        def _():
            load_inv(k).wait()

        qbuf[p] = jnp.dot(resid[s], inv[k], preferred_element_type=jnp.float32)
        theirs = pl.ds(pl.multiple_of((1 - h) * HALF, HALF), HALF)
        pair_s[s] = qbuf[p, theirs, :].astype(jnp.bfloat16)
        pair_copy(s).start()

    def fourth(i):
        k, p, s = split(i)
        pair_copy(s).wait_recv()
        mine = pl.ds(pl.multiple_of(h * HALF, HALF), HALF)
        both = qbuf[p, mine, :] + pair_r[s].astype(jnp.float32)
        qbuf[p, mine, :] = both
        rs_s[s] = both.astype(jnp.bfloat16)
        for d in range(1, M):
            rs_copy(s, d).start()

    def fifth(i):
        k, p, s = split(i)
        rows, lanes = share(h * HALF, m)
        total = qbuf[p, rows, lanes]
        for d in range(1, M):
            rs_copy(s, d).wait_recv()
        for d in range(1, M):
            total = total + rs_r[s, d - 1].astype(jnp.float32)
        rows, lanes = share(p * N + h * HALF, m)
        xt[k, rows, lanes] = total.astype(jnp.bfloat16)
        for d in range(1, M):
            ag_copy(s, k, p, d).start()

    def sixth(i):
        k, p, s = split(i)
        for d in range(1, M):
            ag_copy(s, k, p, d).wait_recv()
        fwd_copy(s, k, p).start()

    def sends(i):
        k, p, s = split(i)
        inner_copy(s).wait_send()

        @pl.when(jnp.logical_not(edge))
        def _():
            back_copy(s).wait_send()

        pair_copy(s).wait_send()
        for d in range(1, M):
            rs_copy(s, d).wait_send()
        for d in range(1, M):
            ag_copy(s, k, p, d).wait_send()
        fwd_copy(s, k, p).wait_send()

    mid_lags = [min(lag, LAG_BASE) * (PC - 1) // LAG_BASE for lag in MID_LAGS]
    end_lags = [min(lag, LAG_BASE) * (PC - 1) // LAG_BASE for lag in END_LAGS]
    stages = list(zip((first, second, third, fourth, fifth, sixth), mid_lags, end_lags))
    stages.append((sends, PC + PC // 2, PC + PC // 2))

    def step(t, carry):
        for stage, mid_lag, end_lag in stages:
            i = t - jnp.where(mid, mid_lag, end_lag)

            @pl.when(jnp.logical_and(i >= 0, i < items))
            def _(stage=stage, i=i):
                stage(i)
        return carry

    lax.fori_loop(0, items + PC + PC // 2, step, 0)

    def last(i, carry):
        k, p, s = split(i)
        fwd_copy(s, k, p).wait_recv()
        return carry

    lax.fori_loop(items - PC, items, last, 0)
    cut = out.shape[2]
    source = xt
    if cut < depth:
        source = xt.at[:, :, pl.ds(pl.multiple_of(c * cut, cut), cut)]
    write = pltpu.make_async_copy(source, out, o_sem)
    write.start()
    write.wait()


def solve(pend, lower, inv, R, C):
    NB, sources, width = pend.shape
    depth = inv.shape[2]
    wide = depth % (64 * C) == 0
    N = min(8 * C if wide else 16 * C, sources // 2)
    PC = sources // N
    S = 2 * PC
    M = C // 2
    bf, f32 = jnp.bfloat16, jnp.float32
    dma = pltpu.SemaphoreType.DMA
    anywhere = pl.BlockSpec(memory_space=pl.ANY)
    cut = depth // C if depth % (128 * C) == 0 else depth
    return pl.pallas_call(
        functools.partial(solve_kernel, (R, C, NB, N, PC)),
        out_shape=jax.ShapeDtypeStruct((NB, sources, cut), bf),
        in_specs=[anywhere, anywhere, anywhere],
        out_specs=pl.BlockSpec(memory_space=pl.ANY),
        scratch_shapes=[
            pltpu.VMEM(pend.shape, f32),
            pltpu.VMEM(lower.shape, bf),
            pltpu.VMEM(inv.shape, bf),
            pltpu.VMEM((NB, sources, depth), bf),
            pltpu.VMEM((PC, N, width), f32),
            pltpu.VMEM((PC, N, depth), f32),
            pltpu.VMEM((S, N, width), bf),
            pltpu.VMEM((S, N, width), bf),
            pltpu.VMEM((S, N, width), bf),
            pltpu.VMEM((S, N, width), bf),
            pltpu.VMEM((S, N // 2, depth), bf),
            pltpu.VMEM((S, N // 2, depth), bf),
            pltpu.VMEM((S, N // 2, depth), bf),
            pltpu.VMEM((S, M - 1) + ((N // 2, depth // M) if N // C < 16 else (N // C, depth)), bf),
            dma((S,)), dma((S,)), dma((S,)), dma((S,)), dma((S,)), dma((S,)), dma((S,)),
            dma((S, M - 1)), dma((S, M - 1)), dma((S, M - 1)), dma((S, M - 1)),
            dma((S,)), dma((S,)), dma, dma((NB,)), dma((NB,)), dma,
        ],
        compiler_params=pltpu.CompilerParams(
            collective_id=0, has_side_effects=True, vmem_limit_bytes=60 * 1024 * 1024
        ),
    )(pend, lower, inv)


def fused_kernel(dims, rhs_in, bound_in, border_in, lower_in, inv_in, owners, out, tiles, raw, bound, pend, rhs, inv, xt,
                 part, qbuf, sbuf, recv_a, xbuf, resid, pair_s, pair_r, rs_s, rs_r, select, own, pack, recv,
                 s_sem, a_sem, x_sem, b_sem, bs_sem, ps_sem, pr_sem, rss_sem, rsr_sem, ags_sem, agr_sem, fs_sem, fr_sem,
                 o_sem, raw_sem, bd_sem, rhs_sem, il_sem, ll_sem, ks_sem, kr_sem):
    R, C, NB, N, PC, S, most = dims
    devices = R * C
    M = C // 2
    HALF = N // 2
    depth = inv.shape[2]
    LW = depth // M
    LB = depth // C
    G, slots, GW = pack.shape
    PG = GW // N
    PB = part.shape[0]
    QB = qbuf.shape[0]
    NR, RB = raw.shape[:2]
    QK = bound.shape[1] // depth
    BW = pend.shape[1]
    GB = PC // QK
    chunks = NB * GB
    blocks_raw = bound.shape[1] // RB
    late = []
    for earlier in range(NB - 2, -1, -1):
        late += [(later, earlier) for later in range(earlier + 1, NB)]
    late_unit = {}
    for n, (later, earlier) in enumerate(late):
        unit = NB * QK if n == 0 else (NB - 1) * QK + n - 1
        if n > QK:
            unit = NB * QK + n - QK
        late_unit[later * (later - 1) // 2 + earlier] = unit
    items = NB * PC
    z = lax.axis_index("rows")
    c = lax.axis_index("cols")
    h = lax.rem(c, 2)
    m = c // 2
    low = z < R // 2
    mid = jnp.logical_or(z == R // 2 - 1, z == R // 2)
    edge = jnp.logical_or(z == 0, z == R - 1)
    inner = jnp.where(low, z + 1, z - 1)
    outer = jnp.where(low, z - 1, z + 1)
    outer_safe = jnp.where(edge, inner, outer)
    partner = c + 1 - 2 * h
    me = z * C + c

    def place(d):
        if M == 4:
            return 2 * lax.rem(m // 2 + d // 2, 2) + lax.rem(m + d, 2)
        return lax.rem(m + d, M)

    def peer(d):
        return 2 * place(d) + h

    def share(base, q):
        return pl.ds(pl.multiple_of(base, HALF), HALF), pl.ds(pl.multiple_of(q * LW, LW), LW)

    def load_inv(k):
        return pltpu.make_async_copy(inv_in.at[k], inv.at[k], il_sem.at[k])

    def load_lower(n):
        pair = late[n][0] * (late[n][0] - 1) // 2 + late[n][1]
        return pltpu.make_async_copy(lower_in.at[pair], tiles.at[late_unit[pair]], ll_sem.at[n])

    def load_raw(e):
        pair = NB // 2 - 1 - e // blocks_raw
        rows = pl.ds(pl.multiple_of(lax.rem(e, blocks_raw) * RB, RB), RB)
        slot = lax.rem(e, NR)
        return pltpu.make_async_copy(border_in.at[rows, pl.ds(2 * pair, 2), :], raw.at[slot], raw_sem.at[slot])

    def load_bound(q):
        return pltpu.make_async_copy(bound_in.at[pl.ds(q * depth, depth)], xt.at[q], bd_sem.at[q])

    def load_rhs(g):
        lanes = pl.ds(pl.multiple_of(g * BW, BW), BW)
        slot = lax.rem(g, 2)
        return pltpu.make_async_copy(rhs_in.at[z, :, lanes], rhs.at[slot], rhs_sem.at[slot])

    def untangle(e):
        pair = NB // 2 - 1 - e // blocks_raw
        start = lax.rem(e, blocks_raw) * RB
        rows = pl.ds(pl.multiple_of(lax.rem(start, depth), RB), RB)
        load_raw(e).wait()
        both = jnp.swapaxes(raw[lax.rem(e, NR)], 0, 1)
        for b in range(2):
            tiles[(2 * pair + b) * QK + start // depth, rows, :] = both[b]

        @pl.when(e + NR < NB // 2 * blocks_raw)
        def _():
            load_raw(e + NR).start()

    def turn(g, q):
        rows = pl.ds(pl.multiple_of(g * BW, BW), BW)
        lanes = pl.ds(pl.multiple_of(q * depth, depth), depth)
        bound[rows, lanes] = xt[q, :, rows].T

    def border(j, half):
        k = NB - 1 - j // GB
        g = lax.rem(j, GB)
        slot = lax.rem(j, 2)
        rows = pl.ds(pl.multiple_of(g * BW, BW), BW)
        width = pend.shape[2]
        lanes = pl.ds(pl.multiple_of(half * (width // 2), width // 2), width // 2)
        block = tiles[pl.ds(k * QK, QK), :, lanes].reshape(QK * depth, width // 2)
        pend[slot, :, lanes] = jnp.dot(bound[rows, :], block, preferred_element_type=jnp.float32)

        @pl.when(jnp.logical_and(half == 1, k == z))
        def _():
            load_rhs(g).wait()
            pend[slot] -= rhs[lax.rem(g, 2)].T

            @pl.when(g + 2 < GB)
            def _():
                load_rhs(g + 2).start()

    def unit_of(pair):
        unit = late_unit[0]
        for n in range(1, len(late)):
            unit = jnp.where(pair == n, late_unit[n], unit)
        return unit

    def ahead(j, half, later):
        k = NB - 1 - j // GB
        rows = pl.ds(pl.multiple_of(lax.rem(j, GB) * BW, BW), BW)
        width = pend.shape[2]
        lanes = pl.ds(pl.multiple_of(half * (width // 2), width // 2), width // 2)
        pend[lax.rem(j, 2), :, lanes] += jnp.dot(
            xt[later, rows, :], tiles[unit_of(later * (later - 1) // 2 + k), :, lanes],
            preferred_element_type=jnp.float32,
        )

    def first_raw(e, carry):
        load_raw(e).start()
        return carry

    lax.fori_loop(0, NR, first_raw, 0)
    order = [QK - 1] + list(range(QK - 1))
    load_bound(order[0]).start()
    load_bound(order[1]).start()
    load_rhs(0).start()
    load_rhs(1).start()
    load_inv(NB - 1).start()

    barrier = pltpu.get_barrier_semaphore()

    def device(d):
        o = lax.rem(me + d, devices)
        return o, {"rows": o // C, "cols": lax.rem(o, C)}

    def greet(d, carry):
        pl.semaphore_signal(barrier, inc=1, device_id=device(d)[1], device_id_type=MESH)
        return carry

    lax.fori_loop(1, devices, greet, 0)
    RC = 128
    FC = slots // 2

    wide = select.shape[1]
    names = owners[...].astype(jnp.float32)
    ranks = jnp.zeros((1, wide), jnp.float32)
    for q in range(0, wide, RC):
        down = q + lax.broadcasted_iota(jnp.int32, (RC, wide), 0)
        over = lax.broadcasted_iota(jnp.int32, (RC, wide), 1)
        column = jnp.sum(jnp.where(down == over, names, 0.0), axis=1, keepdims=True)
        same = jnp.logical_and(column == names, down < over)
        ranks = ranks + jnp.sum(jnp.where(same, 1.0, 0.0), axis=0, keepdims=True)
    target = (names * most + ranks).astype(jnp.int32)

    def choose(q, carry):
        rows = pl.ds(pl.multiple_of(q * RC, RC), RC)
        ids = q * RC + lax.broadcasted_iota(jnp.int32, (RC, wide), 0)
        select[rows, :] = jnp.where(ids == target, 1.0, 0.0).astype(jnp.bfloat16)
        return carry

    lax.fori_loop(0, slots // RC, choose, 0)

    def first_half(e, carry):
        untangle(e)
        return carry

    stretch = blocks_raw // QK
    for n in range(QK):
        lax.fori_loop(n * stretch, (n + 1) * stretch, first_half, 0)
        if n + 2 < QK:
            load_bound(order[n + 2]).start()
        load_bound(order[n]).wait()
        for g in range(GB if n == 0 else 2):
            turn(g, order[n])
    for b in range(NB - 2, -1, -1):
        load_inv(b).start()
    load_lower(0).start()
    border(0, 0)
    border(0, 1)
    pl.semaphore_wait(barrier, devices - 1)

    def remote(src, dst, ss, rs, where):
        return pltpu.make_async_remote_copy(src_ref=src, dst_ref=dst, send_sem=ss, recv_sem=rs,
                                            device_id=where, device_id_type=MESH)

    def inner_copy(s):
        return remote(sbuf.at[s], recv_a.at[s], s_sem.at[s], a_sem.at[s], {"rows": inner})

    def swap_copy(s):
        return remote(sbuf.at[s], xbuf.at[s], s_sem.at[s], x_sem.at[s], {"rows": inner})

    def back_copy(s):
        return remote(resid.at[s], resid.at[s], bs_sem.at[s], b_sem.at[s], {"rows": outer_safe})

    def pair_copy(s):
        return remote(pair_s.at[s], pair_r.at[s], ps_sem.at[s], pr_sem.at[s], {"cols": partner})

    def rs_copy(s, d):
        rows, lanes = share(0, place(d))
        return remote(rs_s.at[s, rows, lanes], rs_r.at[s, d - 1], rss_sem.at[s], rsr_sem.at[s],
                      {"cols": peer(d)})

    def all_of(s, sem):
        return pltpu.make_async_copy(rs_r.at[s], rs_r.at[s], sem.at[s])

    def ag_copy(s, k, p, d):
        rows, lanes = share(p * N + h * HALF, m)
        return remote(xt.at[k, rows, lanes], xt.at[k, rows, lanes], ags_sem.at[s], agr_sem.at[s],
                      {"cols": peer(d)})

    def fwd_copy(s, k, p):
        rows = pl.ds(pl.multiple_of(p * N + h * HALF, HALF), HALF)
        return remote(xt.at[k, rows], xt.at[k, rows], fs_sem.at[s], fr_sem.at[s], {"cols": partner})

    def half_copy(s, p):
        rows = pl.ds(pl.multiple_of(p * N + h * HALF, HALF), HALF)
        lanes = pl.ds(pl.multiple_of(partner * LB, LB), LB)
        return remote(xt.at[0, rows, lanes], xt.at[0, rows, lanes], fs_sem.at[s], fr_sem.at[s], {"cols": partner})

    def section(rows):
        return pl.ds(pl.multiple_of(rows * most, most), most)

    def send_copy(g, d):
        o, where = device(d)
        return remote(pack.at[g, section(o)], recv.at[g, section(me)], ks_sem.at[g], kr_sem.at[g], where)

    def out_copy(g):
        return pltpu.make_async_copy(recv.at[g], out.at[:, pl.ds(pl.multiple_of(g * GW, GW), GW)], o_sem.at[g])

    def split(i):
        k = NB - 1 - i // PC
        return k, lax.rem(i, PC), lax.rem(i, S)

    def piece(p):
        return pl.ds(pl.multiple_of(p * N, N), N)

    def first(i):
        k, p, s = split(i)

        @pl.when(i >= PC)
        def _():
            kb, pb, sb = split(i - PC)
            fwd_copy(sb, kb, pb).wait_recv()

        @pl.when(i == PC)
        def _():
            load_lower(0).wait()

        @pl.when(i == 2 * PC - QK)
        def _():
            for n in range(1, len(late)):
                load_lower(n).wait()

        a = lax.rem(i, PB)
        ready = pl.ds(pl.multiple_of(lax.rem(i, QK) * N, N), N)

        def hold(value):
            @pl.when(edge)
            def _():
                sbuf[s] = value.astype(jnp.bfloat16)
                inner_copy(s).start()

            @pl.when(jnp.logical_not(edge))
            def _():
                part[a] = value

        @pl.when(i < PC)
        def _():
            hold(pend[lax.rem(i // QK, 2), ready, :])

        @pl.when(i >= PC)
        def _():
            j = k + 1
            hold(pend[lax.rem(i // QK, 2), ready, :] + jnp.dot(
                xt[j, piece(p), :], tiles[unit_of(j * (j - 1) // 2 + k)], preferred_element_type=jnp.float32
            ))

    def second(i):
        k, p, s = split(i)

        @pl.when(jnp.logical_not(edge))
        def _():
            a = lax.rem(i, PB)
            inner_copy(s).wait_recv()
            both = part[a] + recv_a[s].astype(jnp.float32)
            part[a] = both
            sbuf[s] = both.astype(jnp.bfloat16)

            @pl.when(mid)
            def _():
                swap_copy(s).start()

            @pl.when(jnp.logical_not(mid))
            def _():
                inner_copy(s).start()

    def third(i):
        k, p, s = split(i)

        @pl.when(mid)
        def _():
            swap_copy(s).wait_recv()
            resid[s] = (-(part[lax.rem(i, PB)] + xbuf[s].astype(jnp.float32))).astype(jnp.bfloat16)

        @pl.when(jnp.logical_not(mid))
        def _():
            back_copy(s).wait_recv()

        @pl.when(jnp.logical_not(edge))
        def _():
            back_copy(s).start()

        @pl.when(p == 0)
        def _():
            load_inv(k).wait()

        terms = jnp.dot(resid[s], inv[k], preferred_element_type=jnp.float32)
        pair_s[s] = jnp.where(h == 0, terms[HALF:], terms[:HALF]).astype(jnp.bfloat16)
        pair_copy(s).start()
        qbuf[lax.rem(i, QB)] = jnp.where(h == 0, terms[:HALF], terms[HALF:])

    def fourth(i):
        k, p, s = split(i)
        pair_copy(s).wait_recv()
        rs_s[s] = (qbuf[lax.rem(i, QB)] + pair_r[s].astype(jnp.float32)).astype(jnp.bfloat16)
        for d in range(M - 1, 0, -1):
            rs_copy(s, d).start()

    def fifth(i):
        k, p, s = split(i)
        lanes = share(0, m)[1]
        total = qbuf[lax.rem(i, QB), :, lanes] + pair_r[s, :, lanes].astype(jnp.float32)
        all_of(s, rsr_sem).wait()
        for d in range(1, M):
            total = total + rs_r[s, d - 1].astype(jnp.float32)
        rows, lanes = share(p * N + h * HALF, m)
        xt[k, rows, lanes] = total.astype(jnp.bfloat16)

        @pl.when(k > 0)
        def _():
            for d in range(M - 1, 0, -1):
                ag_copy(s, k, p, d).start()

        @pl.when(k == 0)
        def _():
            half_copy(s, p).start()

    def sixth(i):
        k, p, s = split(i)

        @pl.when(k > 0)
        def _():
            all_of(s, agr_sem).wait()
            fwd_copy(s, k, p).start()

    def seventh(i):
        k, p, s = split(i)

        @pl.when(k == 0)
        def _():
            half_copy(s, p).wait_recv()

        @pl.when(jnp.logical_and(k == 0, lax.rem(p, PG) == PG - 1))
        def _():
            g = p // PG
            rows = pl.ds(pl.multiple_of(g * GW, GW), GW)
            lanes = pl.ds(pl.multiple_of(c * LB, LB), LB)
            for b in range(NB):
                own[:, b * LB:(b + 1) * LB] = xt[b, rows, lanes]

            def fill(q, carry):
                part_rows = pl.ds(pl.multiple_of(q * FC, FC), FC)
                pack[g, part_rows, :] = lax.dot_general(
                    select[part_rows, :], own[...], (((1,), (1,)), ((), ())), preferred_element_type=jnp.float32
                ).astype(jnp.bfloat16)
                return carry

            lax.fori_loop(0, slots // FC, fill, 0)

            def send(d, carry):
                send_copy(g, d).start()
                return carry

            lax.fori_loop(1, devices, send, 0)
            pltpu.make_async_copy(pack.at[g, section(me)], recv.at[g, section(me)], kr_sem.at[g]).start()

    def sends(i):
        k, p, s = split(i)
        inner_copy(s).wait_send()

        @pl.when(jnp.logical_not(edge))
        def _():
            back_copy(s).wait_send()

        pair_copy(s).wait_send()
        all_of(s, rss_sem).wait()

        @pl.when(k > 0)
        def _():
            all_of(s, ags_sem).wait()
            fwd_copy(s, k, p).wait_send()

        @pl.when(k == 0)
        def _():
            half_copy(s, p).wait_send()

    mid_lags = [min(lag, LAG_BASE) * (PC - 1) // LAG_BASE for lag in MID_LAGS]
    end_lags = [min(lag, LAG_BASE) * (PC - 1) // LAG_BASE for lag in END_LAGS]
    stages = list(zip((first, second, third, fourth, fifth, sixth), mid_lags, end_lags))
    stages.append((seventh, PC - 1, PC - 1))
    stages.append((sends, S - 1, S - 1))

    def fill_in(t):
        @pl.when(t < blocks_raw)
        def _():
            untangle(blocks_raw + t)

        @pl.when(t < QK * (chunks - 1))
        def _():
            j, q = t // QK + 1, lax.rem(t, QK)

            k = NB - 1 - j // GB

            @pl.when(lax.rem(q, 2) == 0)
            def _():
                border(j, q // 2)

            @pl.when(jnp.logical_and(lax.rem(q, 2) == 1, k + 2 < NB))
            def _():
                ahead(j, q // 2, k + 2)

            @pl.when(jnp.logical_and(lax.rem(q, 2) == 1, k + 3 < NB))
            def _():
                ahead(j, q // 2, k + 3)

            @pl.when(jnp.logical_and(j + 1 < GB, q > 0))
            def _():
                turn(j + 1, q - 1)


    def step(t, carry):
        for n, (stage, mid_lag, end_lag) in enumerate(stages):
            if n == 1:
                fill_in(t)
            i = t - jnp.where(mid, mid_lag, end_lag)

            @pl.when(jnp.logical_and(i >= 0, i < items))
            def _(stage=stage, i=i):
                stage(i)

        @pl.when(t == QK * (GB - 1))
        def _():
            for n in range(1, len(late)):
                load_lower(n).start()
        return carry

    lax.fori_loop(0, items + S - 1, step, 0)

    def arrive(g, carry):
        pltpu.make_async_copy(recv.at[g], recv.at[g], kr_sem.at[g]).wait()
        out_copy(g).start()
        return carry

    lax.fori_loop(0, G, arrive, 0)

    def finish(g, carry):
        sent = pack.at[g, pl.ds(0, slots - most)]
        pltpu.make_async_copy(sent, sent, ks_sem.at[g]).wait()
        out_copy(g).wait()
        return carry

    lax.fori_loop(0, G, finish, 0)


def fused(rhs, bound, border, lower, inv, owners, R, C, most):
    NB, width, sources = rhs.shape
    depth = inv.shape[2]
    devices = R * C
    N = 8 * C
    PC = sources // N
    S = PC + 4
    M = C // 2
    GW = GROUP * N
    G = sources // GW
    QK = bound.shape[0] // depth
    pairs = lower.shape[0]
    PB = max(MID_LAGS[2], END_LAGS[2]) + 2
    QB = max(MID_LAGS[4] - MID_LAGS[2], END_LAGS[4] - END_LAGS[2]) + 2
    bf, f32 = jnp.bfloat16, jnp.float32
    dma = pltpu.SemaphoreType.DMA
    anywhere = pl.BlockSpec(memory_space=pl.ANY)
    return pl.pallas_call(
        functools.partial(fused_kernel, (R, C, NB, N, PC, S, most)),
        out_shape=jax.ShapeDtypeStruct((devices * most, sources), bf),
        in_specs=[anywhere] * 5 + [pl.BlockSpec(memory_space=pltpu.VMEM)],
        out_specs=pl.BlockSpec(memory_space=pl.ANY),
        scratch_shapes=[
            pltpu.VMEM((NB * QK + 1 + max(0, pairs - 1 - QK), depth, width), bf),
            pltpu.VMEM((RAW, RAW_ROWS, 2, width), bf),
            pltpu.VMEM((sources, bound.shape[0]), bf),
            pltpu.VMEM((2, QK * N, width), f32),
            pltpu.VMEM((2, width, QK * N), f32),
            pltpu.VMEM(inv.shape, bf),
            pltpu.VMEM((NB, sources, depth), bf),
            pltpu.VMEM((PB, N, width), f32),
            pltpu.VMEM((QB, N // 2, depth), f32),
            pltpu.VMEM((S, N, width), bf),
            pltpu.VMEM((S, N, width), bf),
            pltpu.VMEM((S, N, width), bf),
            pltpu.VMEM((S, N, width), bf),
            pltpu.VMEM((S, N // 2, depth), bf),
            pltpu.VMEM((S, N // 2, depth), bf),
            pltpu.VMEM((S, N // 2, depth), bf),
            pltpu.VMEM((S, M - 1, N // 2, depth // M), bf),
            pltpu.VMEM((devices * most, owners.shape[1]), bf),
            pltpu.VMEM((GW, owners.shape[1]), bf),
            pltpu.VMEM((G, devices * most, GW), bf),
            pltpu.VMEM((G, devices * most, GW), bf),
            dma((S,)), dma((S,)), dma((S,)), dma((S,)), dma((S,)), dma((S,)), dma((S,)),
            dma((S,)), dma((S,)), dma((S,)), dma((S,)),
            dma((S,)), dma((S,)), dma((G,)), dma((RAW,)), dma((QK,)), dma((2,)), dma((NB,)), dma((pairs,)),
            dma((G,)), dma((G,)),
        ],
        compiler_params=pltpu.CompilerParams(
            collective_id=1, has_side_effects=True, vmem_limit_bytes=VMEM_BYTES
        ),
    )(rhs, bound, border, lower, inv, owners)


def widen_kernel(source, out, narrow, full, in_sem, out_sem):
    parts = in_sem.shape[0]
    rows = source.shape[0] // parts

    def take(n):
        part = pl.ds(n * rows, rows)
        return pltpu.make_async_copy(source.at[part], narrow.at[part], in_sem.at[n])

    def give(n):
        part = pl.ds(n * rows, rows)
        return pltpu.make_async_copy(full.at[part], out.at[part], out_sem.at[n])

    for n in range(parts):
        take(n).start()
    for n in range(parts):
        take(n).wait()
        full[n * rows:(n + 1) * rows, :] = narrow[n * rows:(n + 1) * rows, :].astype(jnp.float32)
        give(n).start()
    for n in range(parts):
        give(n).wait()


def widen(values):
    dma = pltpu.SemaphoreType.DMA
    return pl.pallas_call(
        widen_kernel,
        out_shape=jax.ShapeDtypeStruct(values.shape, jnp.float32),
        in_specs=[pl.BlockSpec(memory_space=pl.ANY)],
        out_specs=pl.BlockSpec(memory_space=pl.ANY),
        scratch_shapes=[
            pltpu.VMEM(values.shape, values.dtype), pltpu.VMEM(values.shape, jnp.float32), dma((PARTS,)), dma((PARTS,)),
        ],
    )(values)


def local(pivot_rhs, bound_sol, border_tiles, lower_tiles, inverse_diag, owner_map):
    R = lax.axis_size("rows")
    C = lax.axis_size("cols")
    devices = R * C
    blocks, _, sources = pivot_rhs.shape
    rows_dev = owner_map.shape[1]
    per_block = rows_dev // blocks
    most = max(2, 2 * rows_dev // devices)
    pieces = 8 * C
    depth = inverse_diag.shape[2]
    if (
        R == blocks == 4 and C >= 4 and depth == sources and depth == per_block * C and bound_sol.shape[0] == 4 * depth
        and per_block % 128 == 0 and most % 32 == 0 and sources % (4 * pieces) == 0 and sources == 16 * pieces
        and bound_sol.shape[0] % RAW_ROWS == 0
    ):
        received = fused(
            pivot_rhs, bound_sol, border_tiles, lower_tiles, inverse_diag, owner_map[:, :, 0], R, C, most
        )
        return widen(received)
    border = lax.dot_general(
        bound_sol, border_tiles, (((0,), (0,)), ((), ())), preferred_element_type=jnp.float32
    )
    row = lax.axis_index("rows")
    if R % blocks == 0:
        block = row // (R // blocks)
        mine = jnp.logical_and(jnp.arange(blocks) == block, lax.rem(row, R // blocks) == 0)
        rhs = lax.dynamic_index_in_dim(pivot_rhs, block, 0, keepdims=False).T[None]
        rhs = jnp.where(mine[:, None, None], rhs, 0.0)
    else:
        rhs = jnp.where(row == R // 2 - 1, pivot_rhs.transpose(0, 2, 1), 0.0)
    pend = border.transpose(1, 0, 2) - rhs
    owners = owner_map[0, :, 0]
    onehot = (owners[:, None] == jnp.arange(devices, dtype=jnp.int32)[None, :]).astype(jnp.int32)
    ranks = jnp.cumsum(onehot, axis=0) - onehot
    slots = jnp.sum(ranks * onehot, axis=1)
    target = owners * most + slots
    xt = solve(pend, lower_tiles, inverse_diag, R, C)

    own = xt
    if xt.shape[2] > per_block:
        own = lax.dynamic_slice_in_dim(xt, lax.axis_index("cols") * per_block, per_block, axis=2)
    select = (jnp.arange(devices * most, dtype=jnp.int32)[:, None] == target[None, :]).astype(jnp.bfloat16)
    select = select.reshape(devices * most, blocks, per_block)
    packed = lax.dot_general(
        select, own, (((1, 2), (0, 2)), ((), ())), preferred_element_type=jnp.float32
    ).astype(jnp.bfloat16)
    received = lax.all_to_all(
        packed.reshape(devices, most, sources), ("rows", "cols"), split_axis=0, concat_axis=0, tiled=True
    )
    return received.reshape(devices * most, sources).astype(jnp.float32)


def solution(mesh):
    placed = (
        P(None, "cols", None),
        P("rows", None),
        P("rows", None, "cols"),
        P(None, "rows", "cols"),
        P(None, "cols", "rows"),
        P(("rows", "cols"), None, None),
    )
    return jax.shard_map(
        local, mesh=mesh, in_specs=placed, out_specs=P(("rows", "cols"), None), check_vma=False
    )
```

```python
import functools

import jax
import jax.numpy as jnp
from jax import lax
from jax.experimental import pallas as pl
from jax.experimental.pallas import tpu as pltpu
from jax.sharding import PartitionSpec as P

MESH = pl.DeviceIdType.MESH
MID_LAGS = (0, 3, 6, 8, 11, 14)
END_LAGS = (0, 0, 9, 10, 12, 14)
LAG_BASE = 15
GROUP = 4
RAW = 6
PARTS = 8
RAW_ROWS = 256
VMEM_BYTES = 63 * 1024 * 1024 + 512 * 1024


def solve_kernel(dims, pend_in, lower_in, inv_in, out, pend, lower, inv, xt, part, qbuf, sbuf, recv_a, xbuf, resid,
                 pair_s, pair_r, rs_s, rs_r, s_sem, a_sem, x_sem, b_sem, bs_sem, ps_sem, pr_sem,
                 rss_sem, rsr_sem, ags_sem, agr_sem, fs_sem, fr_sem, o_sem, pl_sem, il_sem, ll_sem):
    R, C, NB, N, PC = dims
    M = C // 2
    HALF = N // 2
    depth = inv.shape[2]
    by_lanes = N // C < 16
    CH = HALF if by_lanes else HALF // M
    LW = depth // M if by_lanes else depth
    S = 2 * PC
    items = NB * PC
    z = lax.axis_index("rows")
    c = lax.axis_index("cols")
    h = lax.rem(c, 2)
    m = c // 2
    low = z < R // 2
    mid = jnp.logical_or(z == R // 2 - 1, z == R // 2)
    edge = jnp.logical_or(z == 0, z == R - 1)
    inner = jnp.where(low, z + 1, z - 1)
    outer = jnp.where(low, z - 1, z + 1)
    outer_safe = jnp.where(edge, inner, outer)
    partner = c + 1 - 2 * h

    def peer(d):
        return 2 * lax.rem(m + d, M) + h

    def share(base, q):
        if by_lanes:
            return pl.ds(pl.multiple_of(base, HALF), HALF), pl.ds(pl.multiple_of(q * LW, LW), LW)
        return pl.ds(pl.multiple_of(base + q * CH, CH), CH), slice(None)

    def load_pend(k):
        return pltpu.make_async_copy(pend_in.at[k], pend.at[k], pl_sem.at[k])

    def load_inv(k):
        return pltpu.make_async_copy(inv_in.at[k], inv.at[k], il_sem.at[k])

    load_lower = pltpu.make_async_copy(lower_in, lower, ll_sem)
    load_pend(NB - 1).start()
    load_inv(NB - 1).start()
    load_lower.start()
    for k in range(NB - 2, -1, -1):
        load_pend(k).start()
        load_inv(k).start()

    barrier = pltpu.get_barrier_semaphore()

    @pl.when(z > 0)
    def _():
        pl.semaphore_signal(barrier, inc=1, device_id={"rows": z - 1}, device_id_type=MESH)

    @pl.when(z < R - 1)
    def _():
        pl.semaphore_signal(barrier, inc=1, device_id={"rows": z + 1}, device_id_type=MESH)

    pl.semaphore_signal(barrier, inc=1, device_id={"cols": partner}, device_id_type=MESH)
    for d in range(1, M):
        pl.semaphore_signal(barrier, inc=1, device_id={"cols": peer(d)}, device_id_type=MESH)
    pl.semaphore_wait(barrier, M + jnp.where(edge, 1, 2))

    def remote(src, dst, ss, rs, where):
        return pltpu.make_async_remote_copy(src_ref=src, dst_ref=dst, send_sem=ss, recv_sem=rs,
                                            device_id=where, device_id_type=MESH)

    def inner_copy(s):
        return remote(sbuf.at[s], recv_a.at[s], s_sem.at[s], a_sem.at[s], {"rows": inner})

    def swap_copy(s):
        return remote(sbuf.at[s], xbuf.at[s], s_sem.at[s], x_sem.at[s], {"rows": inner})

    def back_copy(s):
        return remote(resid.at[s], resid.at[s], bs_sem.at[s], b_sem.at[s], {"rows": outer_safe})

    def pair_copy(s):
        return remote(pair_s.at[s], pair_r.at[s], ps_sem.at[s], pr_sem.at[s], {"cols": partner})

    def rs_copy(s, d):
        rows, lanes = share(0, lax.rem(m + d, M))
        return remote(rs_s.at[s, rows, lanes], rs_r.at[s, d - 1], rss_sem.at[s, d - 1], rsr_sem.at[s, d - 1],
                      {"cols": peer(d)})

    def ag_copy(s, k, p, d):
        rows, lanes = share(p * N + h * HALF, m)
        return remote(xt.at[k, rows, lanes], xt.at[k, rows, lanes], ags_sem.at[s, d - 1], agr_sem.at[s, d - 1],
                      {"cols": peer(d)})

    def fwd_copy(s, k, p):
        rows = pl.ds(pl.multiple_of(p * N + h * HALF, HALF), HALF)
        return remote(xt.at[k, rows], xt.at[k, rows], fs_sem.at[s], fr_sem.at[s], {"cols": partner})

    def split(i):
        k = NB - 1 - i // PC
        return k, lax.rem(i, PC), lax.rem(i, S)

    def piece(p):
        return pl.ds(pl.multiple_of(p * N, N), N)

    def first(i):
        k, p, s = split(i)

        @pl.when(i >= PC)
        def _():
            kb, pb, sb = split(i - PC)
            fwd_copy(sb, kb, pb).wait_recv()

        @pl.when(p == 0)
        def _():
            load_pend(k).wait()

        @pl.when(i == PC)
        def _():
            load_lower.wait()

        part[p] = pend[k, piece(p), :]

        def add(j, carry):
            part[p] += jnp.dot(xt[j, piece(p), :], lower[j * (j - 1) // 2 + k],
                               preferred_element_type=jnp.float32)
            return carry

        lax.fori_loop(k + 1, NB, add, 0)

        @pl.when(edge)
        def _():
            sbuf[s] = part[p].astype(jnp.bfloat16)
            inner_copy(s).start()

    def second(i):
        k, p, s = split(i)

        @pl.when(jnp.logical_not(edge))
        def _():
            inner_copy(s).wait_recv()
            part[p] += recv_a[s].astype(jnp.float32)
            sbuf[s] = part[p].astype(jnp.bfloat16)

            @pl.when(mid)
            def _():
                swap_copy(s).start()

            @pl.when(jnp.logical_not(mid))
            def _():
                inner_copy(s).start()

    def third(i):
        k, p, s = split(i)

        @pl.when(mid)
        def _():
            swap_copy(s).wait_recv()
            resid[s] = (-(part[p] + xbuf[s].astype(jnp.float32))).astype(jnp.bfloat16)

        @pl.when(jnp.logical_not(mid))
        def _():
            back_copy(s).wait_recv()

        @pl.when(jnp.logical_not(edge))
        def _():
            back_copy(s).start()

        @pl.when(p == 0)
        def _():
            load_inv(k).wait()

        qbuf[p] = jnp.dot(resid[s], inv[k], preferred_element_type=jnp.float32)
        theirs = pl.ds(pl.multiple_of((1 - h) * HALF, HALF), HALF)
        pair_s[s] = qbuf[p, theirs, :].astype(jnp.bfloat16)
        pair_copy(s).start()

    def fourth(i):
        k, p, s = split(i)
        pair_copy(s).wait_recv()
        mine = pl.ds(pl.multiple_of(h * HALF, HALF), HALF)
        both = qbuf[p, mine, :] + pair_r[s].astype(jnp.float32)
        qbuf[p, mine, :] = both
        rs_s[s] = both.astype(jnp.bfloat16)
        for d in range(1, M):
            rs_copy(s, d).start()

    def fifth(i):
        k, p, s = split(i)
        rows, lanes = share(h * HALF, m)
        total = qbuf[p, rows, lanes]
        for d in range(1, M):
            rs_copy(s, d).wait_recv()
        for d in range(1, M):
            total = total + rs_r[s, d - 1].astype(jnp.float32)
        rows, lanes = share(p * N + h * HALF, m)
        xt[k, rows, lanes] = total.astype(jnp.bfloat16)
        for d in range(1, M):
            ag_copy(s, k, p, d).start()

    def sixth(i):
        k, p, s = split(i)
        for d in range(1, M):
            ag_copy(s, k, p, d).wait_recv()
        fwd_copy(s, k, p).start()

    def sends(i):
        k, p, s = split(i)
        inner_copy(s).wait_send()

        @pl.when(jnp.logical_not(edge))
        def _():
            back_copy(s).wait_send()

        pair_copy(s).wait_send()
        for d in range(1, M):
            rs_copy(s, d).wait_send()
        for d in range(1, M):
            ag_copy(s, k, p, d).wait_send()
        fwd_copy(s, k, p).wait_send()

    mid_lags = [min(lag, LAG_BASE) * (PC - 1) // LAG_BASE for lag in MID_LAGS]
    end_lags = [min(lag, LAG_BASE) * (PC - 1) // LAG_BASE for lag in END_LAGS]
    stages = list(zip((first, second, third, fourth, fifth, sixth), mid_lags, end_lags))
    stages.append((sends, PC + PC // 2, PC + PC // 2))

    def step(t, carry):
        for stage, mid_lag, end_lag in stages:
            i = t - jnp.where(mid, mid_lag, end_lag)

            @pl.when(jnp.logical_and(i >= 0, i < items))
            def _(stage=stage, i=i):
                stage(i)
        return carry

    lax.fori_loop(0, items + PC + PC // 2, step, 0)

    def last(i, carry):
        k, p, s = split(i)
        fwd_copy(s, k, p).wait_recv()
        return carry

    lax.fori_loop(items - PC, items, last, 0)
    cut = out.shape[2]
    source = xt
    if cut < depth:
        source = xt.at[:, :, pl.ds(pl.multiple_of(c * cut, cut), cut)]
    write = pltpu.make_async_copy(source, out, o_sem)
    write.start()
    write.wait()


def solve(pend, lower, inv, R, C):
    NB, sources, width = pend.shape
    depth = inv.shape[2]
    wide = depth % (64 * C) == 0
    N = min(8 * C if wide else 16 * C, sources // 2)
    PC = sources // N
    S = 2 * PC
    M = C // 2
    bf, f32 = jnp.bfloat16, jnp.float32
    dma = pltpu.SemaphoreType.DMA
    anywhere = pl.BlockSpec(memory_space=pl.ANY)
    cut = depth // C if depth % (128 * C) == 0 else depth
    return pl.pallas_call(
        functools.partial(solve_kernel, (R, C, NB, N, PC)),
        out_shape=jax.ShapeDtypeStruct((NB, sources, cut), bf),
        in_specs=[anywhere, anywhere, anywhere],
        out_specs=pl.BlockSpec(memory_space=pl.ANY),
        scratch_shapes=[
            pltpu.VMEM(pend.shape, f32),
            pltpu.VMEM(lower.shape, bf),
            pltpu.VMEM(inv.shape, bf),
            pltpu.VMEM((NB, sources, depth), bf),
            pltpu.VMEM((PC, N, width), f32),
            pltpu.VMEM((PC, N, depth), f32),
            pltpu.VMEM((S, N, width), bf),
            pltpu.VMEM((S, N, width), bf),
            pltpu.VMEM((S, N, width), bf),
            pltpu.VMEM((S, N, width), bf),
            pltpu.VMEM((S, N // 2, depth), bf),
            pltpu.VMEM((S, N // 2, depth), bf),
            pltpu.VMEM((S, N // 2, depth), bf),
            pltpu.VMEM((S, M - 1) + ((N // 2, depth // M) if N // C < 16 else (N // C, depth)), bf),
            dma((S,)), dma((S,)), dma((S,)), dma((S,)), dma((S,)), dma((S,)), dma((S,)),
            dma((S, M - 1)), dma((S, M - 1)), dma((S, M - 1)), dma((S, M - 1)),
            dma((S,)), dma((S,)), dma, dma((NB,)), dma((NB,)), dma,
        ],
        compiler_params=pltpu.CompilerParams(
            collective_id=0, has_side_effects=True, vmem_limit_bytes=60 * 1024 * 1024
        ),
    )(pend, lower, inv)


def fused_kernel(dims, rhs_in, bound_in, border_in, lower_in, inv_in, owners, out, tiles, raw, bound, pend, rhs, inv, xt,
                 part, qbuf, sbuf, recv_a, xbuf, resid, pair_s, pair_r, rs_s, rs_r, select, own, pack, recv,
                 s_sem, a_sem, x_sem, b_sem, bs_sem, ps_sem, pr_sem, rss_sem, rsr_sem, ags_sem, agr_sem, fs_sem, fr_sem,
                 o_sem, raw_sem, bd_sem, rhs_sem, il_sem, ll_sem, ks_sem, kr_sem):
    R, C, NB, N, PC, S, most = dims
    devices = R * C
    M = C // 2
    HALF = N // 2
    depth = inv.shape[2]
    LW = depth // M
    LB = depth // C
    G, slots, GW = pack.shape
    PG = GW // N
    PB = part.shape[0]
    QB = qbuf.shape[0]
    NR, RB = raw.shape[:2]
    QK = bound.shape[1] // depth
    BW = pend.shape[1]
    GB = PC // QK
    chunks = NB * GB
    blocks_raw = bound.shape[1] // RB
    late = []
    for earlier in range(NB - 2, -1, -1):
        late += [(later, earlier) for later in range(earlier + 1, NB)]
    late_unit = {}
    for n, (later, earlier) in enumerate(late):
        unit = NB * QK if n == 0 else (NB - 1) * QK + n - 1
        if n > QK:
            unit = NB * QK + n - QK
        late_unit[later * (later - 1) // 2 + earlier] = unit
    items = NB * PC
    z = lax.axis_index("rows")
    c = lax.axis_index("cols")
    h = lax.rem(c, 2)
    m = c // 2
    low = z < R // 2
    mid = jnp.logical_or(z == R // 2 - 1, z == R // 2)
    edge = jnp.logical_or(z == 0, z == R - 1)
    inner = jnp.where(low, z + 1, z - 1)
    outer = jnp.where(low, z - 1, z + 1)
    outer_safe = jnp.where(edge, inner, outer)
    partner = c + 1 - 2 * h
    me = z * C + c

    def place(d):
        if M == 4:
            return 2 * lax.rem(m // 2 + d // 2, 2) + lax.rem(m + d, 2)
        return lax.rem(m + d, M)

    def peer(d):
        return 2 * place(d) + h

    def share(base, q):
        return pl.ds(pl.multiple_of(base, HALF), HALF), pl.ds(pl.multiple_of(q * LW, LW), LW)

    def load_inv(k):
        return pltpu.make_async_copy(inv_in.at[k], inv.at[k], il_sem.at[k])

    def load_lower(n):
        pair = late[n][0] * (late[n][0] - 1) // 2 + late[n][1]
        return pltpu.make_async_copy(lower_in.at[pair], tiles.at[late_unit[pair]], ll_sem.at[n])

    def load_raw(e):
        pair = NB // 2 - 1 - e // blocks_raw
        rows = pl.ds(pl.multiple_of(lax.rem(e, blocks_raw) * RB, RB), RB)
        slot = lax.rem(e, NR)
        return pltpu.make_async_copy(border_in.at[rows, pl.ds(2 * pair, 2), :], raw.at[slot], raw_sem.at[slot])

    def load_bound(q):
        return pltpu.make_async_copy(bound_in.at[pl.ds(q * depth, depth)], xt.at[q], bd_sem.at[q])

    def load_rhs(g):
        lanes = pl.ds(pl.multiple_of(g * BW, BW), BW)
        slot = lax.rem(g, 2)
        return pltpu.make_async_copy(rhs_in.at[z, :, lanes], rhs.at[slot], rhs_sem.at[slot])

    def untangle(e):
        pair = NB // 2 - 1 - e // blocks_raw
        start = lax.rem(e, blocks_raw) * RB
        rows = pl.ds(pl.multiple_of(lax.rem(start, depth), RB), RB)
        load_raw(e).wait()
        both = jnp.swapaxes(raw[lax.rem(e, NR)], 0, 1)
        for b in range(2):
            tiles[(2 * pair + b) * QK + start // depth, rows, :] = both[b]

        @pl.when(e + NR < NB // 2 * blocks_raw)
        def _():
            load_raw(e + NR).start()

    def turn(g, q):
        rows = pl.ds(pl.multiple_of(g * BW, BW), BW)
        lanes = pl.ds(pl.multiple_of(q * depth, depth), depth)
        bound[rows, lanes] = xt[q, :, rows].T

    def border(j, half):
        k = NB - 1 - j // GB
        g = lax.rem(j, GB)
        slot = lax.rem(j, 2)
        rows = pl.ds(pl.multiple_of(g * BW, BW), BW)
        width = pend.shape[2]
        lanes = pl.ds(pl.multiple_of(half * (width // 2), width // 2), width // 2)
        block = tiles[pl.ds(k * QK, QK), :, lanes].reshape(QK * depth, width // 2)
        pend[slot, :, lanes] = jnp.dot(bound[rows, :], block, preferred_element_type=jnp.float32)

        @pl.when(jnp.logical_and(half == 1, k == z))
        def _():
            load_rhs(g).wait()
            pend[slot] -= rhs[lax.rem(g, 2)].T

            @pl.when(g + 2 < GB)
            def _():
                load_rhs(g + 2).start()

    def unit_of(pair):
        unit = late_unit[0]
        for n in range(1, len(late)):
            unit = jnp.where(pair == n, late_unit[n], unit)
        return unit

    def ahead(j, half, later):
        k = NB - 1 - j // GB
        rows = pl.ds(pl.multiple_of(lax.rem(j, GB) * BW, BW), BW)
        width = pend.shape[2]
        lanes = pl.ds(pl.multiple_of(half * (width // 2), width // 2), width // 2)
        pend[lax.rem(j, 2), :, lanes] += jnp.dot(
            xt[later, rows, :], tiles[unit_of(later * (later - 1) // 2 + k), :, lanes],
            preferred_element_type=jnp.float32,
        )

    def first_raw(e, carry):
        load_raw(e).start()
        return carry

    lax.fori_loop(0, NR, first_raw, 0)
    order = [QK - 1] + list(range(QK - 1))
    load_bound(order[0]).start()
    load_bound(order[1]).start()
    load_rhs(0).start()
    load_rhs(1).start()
    load_inv(NB - 1).start()

    barrier = pltpu.get_barrier_semaphore()

    def device(d):
        o = lax.rem(me + d, devices)
        return o, {"rows": o // C, "cols": lax.rem(o, C)}

    def greet(d, carry):
        pl.semaphore_signal(barrier, inc=1, device_id=device(d)[1], device_id_type=MESH)
        return carry

    lax.fori_loop(1, devices, greet, 0)
    RC = 128
    FC = slots // 2

    wide = select.shape[1]
    names = owners[...].astype(jnp.float32)
    ranks = jnp.zeros((1, wide), jnp.float32)
    for q in range(0, wide, RC):
        down = q + lax.broadcasted_iota(jnp.int32, (RC, wide), 0)
        over = lax.broadcasted_iota(jnp.int32, (RC, wide), 1)
        column = jnp.sum(jnp.where(down == over, names, 0.0), axis=1, keepdims=True)
        same = jnp.logical_and(column == names, down < over)
        ranks = ranks + jnp.sum(jnp.where(same, 1.0, 0.0), axis=0, keepdims=True)
    target = (names * most + ranks).astype(jnp.int32)

    def choose(q, carry):
        rows = pl.ds(pl.multiple_of(q * RC, RC), RC)
        ids = q * RC + lax.broadcasted_iota(jnp.int32, (RC, wide), 0)
        select[rows, :] = jnp.where(ids == target, 1.0, 0.0).astype(jnp.bfloat16)
        return carry

    lax.fori_loop(0, slots // RC, choose, 0)

    def first_half(e, carry):
        untangle(e)
        return carry

    stretch = blocks_raw // QK
    for n in range(QK):
        lax.fori_loop(n * stretch, (n + 1) * stretch, first_half, 0)
        if n + 2 < QK:
            load_bound(order[n + 2]).start()
        load_bound(order[n]).wait()
        for g in range(GB if n == 0 else 2):
            turn(g, order[n])
    for b in range(NB - 2, -1, -1):
        load_inv(b).start()
    load_lower(0).start()
    border(0, 0)
    border(0, 1)
    pl.semaphore_wait(barrier, devices - 1)

    def remote(src, dst, ss, rs, where):
        return pltpu.make_async_remote_copy(src_ref=src, dst_ref=dst, send_sem=ss, recv_sem=rs,
                                            device_id=where, device_id_type=MESH)

    def inner_copy(s):
        return remote(sbuf.at[s], recv_a.at[s], s_sem.at[s], a_sem.at[s], {"rows": inner})

    def swap_copy(s):
        return remote(sbuf.at[s], xbuf.at[s], s_sem.at[s], x_sem.at[s], {"rows": inner})

    def back_copy(s):
        return remote(resid.at[s], resid.at[s], bs_sem.at[s], b_sem.at[s], {"rows": outer_safe})

    def pair_copy(s):
        return remote(pair_s.at[s], pair_r.at[s], ps_sem.at[s], pr_sem.at[s], {"cols": partner})

    def rs_copy(s, d):
        rows, lanes = share(0, place(d))
        return remote(rs_s.at[s, rows, lanes], rs_r.at[s, d - 1], rss_sem.at[s], rsr_sem.at[s],
                      {"cols": peer(d)})

    def all_of(s, sem):
        return pltpu.make_async_copy(rs_r.at[s], rs_r.at[s], sem.at[s])

    def ag_copy(s, k, p, d):
        rows, lanes = share(p * N + h * HALF, m)
        return remote(xt.at[k, rows, lanes], xt.at[k, rows, lanes], ags_sem.at[s], agr_sem.at[s],
                      {"cols": peer(d)})

    def fwd_copy(s, k, p):
        rows = pl.ds(pl.multiple_of(p * N + h * HALF, HALF), HALF)
        return remote(xt.at[k, rows], xt.at[k, rows], fs_sem.at[s], fr_sem.at[s], {"cols": partner})

    def half_copy(s, p):
        rows = pl.ds(pl.multiple_of(p * N + h * HALF, HALF), HALF)
        lanes = pl.ds(pl.multiple_of(partner * LB, LB), LB)
        return remote(xt.at[0, rows, lanes], xt.at[0, rows, lanes], fs_sem.at[s], fr_sem.at[s], {"cols": partner})

    def section(rows):
        return pl.ds(pl.multiple_of(rows * most, most), most)

    def send_copy(g, d):
        o, where = device(d)
        return remote(pack.at[g, section(o)], recv.at[g, section(me)], ks_sem.at[g], kr_sem.at[g], where)

    def out_copy(g):
        return pltpu.make_async_copy(recv.at[g], out.at[:, pl.ds(pl.multiple_of(g * GW, GW), GW)], o_sem.at[g])

    def split(i):
        k = NB - 1 - i // PC
        return k, lax.rem(i, PC), lax.rem(i, S)

    def piece(p):
        return pl.ds(pl.multiple_of(p * N, N), N)

    def first(i):
        k, p, s = split(i)

        @pl.when(i >= PC)
        def _():
            kb, pb, sb = split(i - PC)
            fwd_copy(sb, kb, pb).wait_recv()

        @pl.when(i == PC)
        def _():
            load_lower(0).wait()

        @pl.when(i == 2 * PC - QK)
        def _():
            for n in range(1, len(late)):
                load_lower(n).wait()

        a = lax.rem(i, PB)
        ready = pl.ds(pl.multiple_of(lax.rem(i, QK) * N, N), N)

        def hold(value):
            @pl.when(edge)
            def _():
                sbuf[s] = value.astype(jnp.bfloat16)
                inner_copy(s).start()

            @pl.when(jnp.logical_not(edge))
            def _():
                part[a] = value

        @pl.when(i < PC)
        def _():
            hold(pend[lax.rem(i // QK, 2), ready, :])

        @pl.when(i >= PC)
        def _():
            j = k + 1
            hold(pend[lax.rem(i // QK, 2), ready, :] + jnp.dot(
                xt[j, piece(p), :], tiles[unit_of(j * (j - 1) // 2 + k)], preferred_element_type=jnp.float32
            ))

    def second(i):
        k, p, s = split(i)

        @pl.when(jnp.logical_not(edge))
        def _():
            a = lax.rem(i, PB)
            inner_copy(s).wait_recv()
            both = part[a] + recv_a[s].astype(jnp.float32)
            part[a] = both
            sbuf[s] = both.astype(jnp.bfloat16)

            @pl.when(mid)
            def _():
                swap_copy(s).start()

            @pl.when(jnp.logical_not(mid))
            def _():
                inner_copy(s).start()

    def third(i):
        k, p, s = split(i)

        @pl.when(mid)
        def _():
            swap_copy(s).wait_recv()
            resid[s] = (-(part[lax.rem(i, PB)] + xbuf[s].astype(jnp.float32))).astype(jnp.bfloat16)

        @pl.when(jnp.logical_not(mid))
        def _():
            back_copy(s).wait_recv()

        @pl.when(jnp.logical_not(edge))
        def _():
            back_copy(s).start()

        @pl.when(p == 0)
        def _():
            load_inv(k).wait()

        terms = jnp.dot(resid[s], inv[k], preferred_element_type=jnp.float32)
        pair_s[s] = jnp.where(h == 0, terms[HALF:], terms[:HALF]).astype(jnp.bfloat16)
        pair_copy(s).start()
        qbuf[lax.rem(i, QB)] = jnp.where(h == 0, terms[:HALF], terms[HALF:])

    def fourth(i):
        k, p, s = split(i)
        pair_copy(s).wait_recv()
        rs_s[s] = (qbuf[lax.rem(i, QB)] + pair_r[s].astype(jnp.float32)).astype(jnp.bfloat16)
        for d in range(M - 1, 0, -1):
            rs_copy(s, d).start()

    def fifth(i):
        k, p, s = split(i)
        lanes = share(0, m)[1]
        total = qbuf[lax.rem(i, QB), :, lanes] + pair_r[s, :, lanes].astype(jnp.float32)
        all_of(s, rsr_sem).wait()
        for d in range(1, M):
            total = total + rs_r[s, d - 1].astype(jnp.float32)
        rows, lanes = share(p * N + h * HALF, m)
        xt[k, rows, lanes] = total.astype(jnp.bfloat16)

        @pl.when(k > 0)
        def _():
            for d in range(M - 1, 0, -1):
                ag_copy(s, k, p, d).start()

        @pl.when(k == 0)
        def _():
            half_copy(s, p).start()

    def sixth(i):
        k, p, s = split(i)

        @pl.when(k > 0)
        def _():
            all_of(s, agr_sem).wait()
            fwd_copy(s, k, p).start()

    def seventh(i):
        k, p, s = split(i)

        @pl.when(k == 0)
        def _():
            half_copy(s, p).wait_recv()

        @pl.when(jnp.logical_and(k == 0, lax.rem(p, PG) == PG - 1))
        def _():
            g = p // PG
            rows = pl.ds(pl.multiple_of(g * GW, GW), GW)
            lanes = pl.ds(pl.multiple_of(c * LB, LB), LB)
            for b in range(NB):
                own[:, b * LB:(b + 1) * LB] = xt[b, rows, lanes]

            def fill(q, carry):
                part_rows = pl.ds(pl.multiple_of(q * FC, FC), FC)
                pack[g, part_rows, :] = lax.dot_general(
                    select[part_rows, :], own[...], (((1,), (1,)), ((), ())), preferred_element_type=jnp.float32
                ).astype(jnp.bfloat16)
                return carry

            lax.fori_loop(0, slots // FC, fill, 0)

            def send(d, carry):
                send_copy(g, d).start()
                return carry

            lax.fori_loop(1, devices, send, 0)
            pltpu.make_async_copy(pack.at[g, section(me)], recv.at[g, section(me)], kr_sem.at[g]).start()

    def sends(i):
        k, p, s = split(i)
        inner_copy(s).wait_send()

        @pl.when(jnp.logical_not(edge))
        def _():
            back_copy(s).wait_send()

        pair_copy(s).wait_send()
        all_of(s, rss_sem).wait()

        @pl.when(k > 0)
        def _():
            all_of(s, ags_sem).wait()
            fwd_copy(s, k, p).wait_send()

        @pl.when(k == 0)
        def _():
            half_copy(s, p).wait_send()

    mid_lags = [min(lag, LAG_BASE) * (PC - 1) // LAG_BASE for lag in MID_LAGS]
    end_lags = [min(lag, LAG_BASE) * (PC - 1) // LAG_BASE for lag in END_LAGS]
    stages = list(zip((first, second, third, fourth, fifth, sixth), mid_lags, end_lags))
    stages.append((seventh, end_lags[4] + 1, end_lags[4] + 1))
    stages.append((sends, S - 1, S - 1))

    def fill_in(t):
        @pl.when(t < blocks_raw)
        def _():
            untangle(blocks_raw + t)

        @pl.when(t < QK * (chunks - 1))
        def _():
            j, q = t // QK + 1, lax.rem(t, QK)

            k = NB - 1 - j // GB

            @pl.when(lax.rem(q, 2) == 0)
            def _():
                border(j, q // 2)

            @pl.when(jnp.logical_and(lax.rem(q, 2) == 1, k + 2 < NB))
            def _():
                ahead(j, q // 2, k + 2)

            @pl.when(jnp.logical_and(lax.rem(q, 2) == 1, k + 3 < NB))
            def _():
                ahead(j, q // 2, k + 3)

            @pl.when(jnp.logical_and(j + 1 < GB, q > 0))
            def _():
                turn(j + 1, q - 1)


    def step(t, carry):
        for n, (stage, mid_lag, end_lag) in enumerate(stages):
            if n == 1:
                fill_in(t)
            i = t - jnp.where(mid, mid_lag, end_lag)

            @pl.when(jnp.logical_and(i >= 0, i < items))
            def _(stage=stage, i=i):
                stage(i)

        @pl.when(t == QK * (GB - 1))
        def _():
            for n in range(1, len(late)):
                load_lower(n).start()
        return carry

    lax.fori_loop(0, items + S - 1, step, 0)

    def arrive(g, carry):
        pltpu.make_async_copy(recv.at[g], recv.at[g], kr_sem.at[g]).wait()
        out_copy(g).start()
        return carry

    lax.fori_loop(0, G, arrive, 0)

    def finish(g, carry):
        sent = pack.at[g, pl.ds(0, slots - most)]
        pltpu.make_async_copy(sent, sent, ks_sem.at[g]).wait()
        out_copy(g).wait()
        return carry

    lax.fori_loop(0, G, finish, 0)


def fused(rhs, bound, border, lower, inv, owners, R, C, most):
    NB, width, sources = rhs.shape
    depth = inv.shape[2]
    devices = R * C
    N = 8 * C
    PC = sources // N
    S = PC + 4
    M = C // 2
    GW = GROUP * N
    G = sources // GW
    QK = bound.shape[0] // depth
    pairs = lower.shape[0]
    PB = max(MID_LAGS[2], END_LAGS[2]) + 2
    QB = max(MID_LAGS[4] - MID_LAGS[2], END_LAGS[4] - END_LAGS[2]) + 2
    bf, f32 = jnp.bfloat16, jnp.float32
    dma = pltpu.SemaphoreType.DMA
    anywhere = pl.BlockSpec(memory_space=pl.ANY)
    return pl.pallas_call(
        functools.partial(fused_kernel, (R, C, NB, N, PC, S, most)),
        out_shape=jax.ShapeDtypeStruct((devices * most, sources), bf),
        in_specs=[anywhere] * 5 + [pl.BlockSpec(memory_space=pltpu.VMEM)],
        out_specs=pl.BlockSpec(memory_space=pl.ANY),
        scratch_shapes=[
            pltpu.VMEM((NB * QK + 1 + max(0, pairs - 1 - QK), depth, width), bf),
            pltpu.VMEM((RAW, RAW_ROWS, 2, width), bf),
            pltpu.VMEM((sources, bound.shape[0]), bf),
            pltpu.VMEM((2, QK * N, width), f32),
            pltpu.VMEM((2, width, QK * N), f32),
            pltpu.VMEM(inv.shape, bf),
            pltpu.VMEM((NB, sources, depth), bf),
            pltpu.VMEM((PB, N, width), f32),
            pltpu.VMEM((QB, N // 2, depth), f32),
            pltpu.VMEM((S, N, width), bf),
            pltpu.VMEM((S, N, width), bf),
            pltpu.VMEM((S, N, width), bf),
            pltpu.VMEM((S, N, width), bf),
            pltpu.VMEM((S, N // 2, depth), bf),
            pltpu.VMEM((S, N // 2, depth), bf),
            pltpu.VMEM((S, N // 2, depth), bf),
            pltpu.VMEM((S, M - 1, N // 2, depth // M), bf),
            pltpu.VMEM((devices * most, owners.shape[1]), bf),
            pltpu.VMEM((GW, owners.shape[1]), bf),
            pltpu.VMEM((G, devices * most, GW), bf),
            pltpu.VMEM((G, devices * most, GW), bf),
            dma((S,)), dma((S,)), dma((S,)), dma((S,)), dma((S,)), dma((S,)), dma((S,)),
            dma((S,)), dma((S,)), dma((S,)), dma((S,)),
            dma((S,)), dma((S,)), dma((G,)), dma((RAW,)), dma((QK,)), dma((2,)), dma((NB,)), dma((pairs,)),
            dma((G,)), dma((G,)),
        ],
        compiler_params=pltpu.CompilerParams(
            collective_id=1, has_side_effects=True, vmem_limit_bytes=VMEM_BYTES
        ),
    )(rhs, bound, border, lower, inv, owners)


def widen_kernel(source, out, narrow, full, in_sem, out_sem):
    parts = in_sem.shape[0]
    rows = source.shape[0] // parts

    def take(n):
        part = pl.ds(n * rows, rows)
        return pltpu.make_async_copy(source.at[part], narrow.at[part], in_sem.at[n])

    def give(n):
        part = pl.ds(n * rows, rows)
        return pltpu.make_async_copy(full.at[part], out.at[part], out_sem.at[n])

    for n in range(parts):
        take(n).start()
    for n in range(parts):
        take(n).wait()
        full[n * rows:(n + 1) * rows, :] = narrow[n * rows:(n + 1) * rows, :].astype(jnp.float32)
        give(n).start()
    for n in range(parts):
        give(n).wait()


def widen(values):
    dma = pltpu.SemaphoreType.DMA
    return pl.pallas_call(
        widen_kernel,
        out_shape=jax.ShapeDtypeStruct(values.shape, jnp.float32),
        in_specs=[pl.BlockSpec(memory_space=pl.ANY)],
        out_specs=pl.BlockSpec(memory_space=pl.ANY),
        scratch_shapes=[
            pltpu.VMEM(values.shape, values.dtype), pltpu.VMEM(values.shape, jnp.float32), dma((PARTS,)), dma((PARTS,)),
        ],
    )(values)


def local(pivot_rhs, bound_sol, border_tiles, lower_tiles, inverse_diag, owner_map):
    R = lax.axis_size("rows")
    C = lax.axis_size("cols")
    devices = R * C
    blocks, _, sources = pivot_rhs.shape
    rows_dev = owner_map.shape[1]
    per_block = rows_dev // blocks
    most = max(2, 2 * rows_dev // devices)
    pieces = 8 * C
    depth = inverse_diag.shape[2]
    if (
        R == blocks == 4 and C >= 4 and depth == sources and depth == per_block * C and bound_sol.shape[0] == 4 * depth
        and per_block % 128 == 0 and most % 32 == 0 and sources % (4 * pieces) == 0 and sources == 16 * pieces
        and bound_sol.shape[0] % RAW_ROWS == 0
    ):
        received = fused(
            pivot_rhs, bound_sol, border_tiles, lower_tiles, inverse_diag, owner_map[:, :, 0], R, C, most
        )
        return widen(received)
    border = lax.dot_general(
        bound_sol, border_tiles, (((0,), (0,)), ((), ())), preferred_element_type=jnp.float32
    )
    row = lax.axis_index("rows")
    if R % blocks == 0:
        block = row // (R // blocks)
        mine = jnp.logical_and(jnp.arange(blocks) == block, lax.rem(row, R // blocks) == 0)
        rhs = lax.dynamic_index_in_dim(pivot_rhs, block, 0, keepdims=False).T[None]
        rhs = jnp.where(mine[:, None, None], rhs, 0.0)
    else:
        rhs = jnp.where(row == R // 2 - 1, pivot_rhs.transpose(0, 2, 1), 0.0)
    pend = border.transpose(1, 0, 2) - rhs
    owners = owner_map[0, :, 0]
    onehot = (owners[:, None] == jnp.arange(devices, dtype=jnp.int32)[None, :]).astype(jnp.int32)
    ranks = jnp.cumsum(onehot, axis=0) - onehot
    slots = jnp.sum(ranks * onehot, axis=1)
    target = owners * most + slots
    xt = solve(pend, lower_tiles, inverse_diag, R, C)

    own = xt
    if xt.shape[2] > per_block:
        own = lax.dynamic_slice_in_dim(xt, lax.axis_index("cols") * per_block, per_block, axis=2)
    select = (jnp.arange(devices * most, dtype=jnp.int32)[:, None] == target[None, :]).astype(jnp.bfloat16)
    select = select.reshape(devices * most, blocks, per_block)
    packed = lax.dot_general(
        select, own, (((1, 2), (0, 2)), ((), ())), preferred_element_type=jnp.float32
    ).astype(jnp.bfloat16)
    received = lax.all_to_all(
        packed.reshape(devices, most, sources), ("rows", "cols"), split_axis=0, concat_axis=0, tiled=True
    )
    return received.reshape(devices * most, sources).astype(jnp.float32)


def solution(mesh):
    placed = (
        P(None, "cols", None),
        P("rows", None),
        P("rows", None, "cols"),
        P(None, "rows", "cols"),
        P(None, "cols", "rows"),
        P(("rows", "cols"), None, None),
    )
    return jax.shard_map(
        local, mesh=mesh, in_specs=placed, out_specs=P(("rows", "cols"), None), check_vma=False
    )
```
